32 devices in a mesh: rows: 16 (over z, y, x), cols: 2 (over core).
Axes of the slice: x: 2, y: 2, z: 4, core: 2. Of those that a mesh axis runs over, the one named last changes fastest.
Arguments:
- pair_map: bfloat16 [32, 128, 2048], P(None, 'cols', 'rows'), may hold values from -44 to 44
- conv_in: bfloat16 [32, 288], replicated, may hold values from -0.375 to 0.375
- embed_weight: bfloat16 [2048, 256], replicated, may hold values from -0.125 to 0.125
- qkv_weight: bfloat16 [256, 768], replicated, may hold values from -0.5 to 0.5
- key_bias: bfloat16 [256, 16, 8], P('rows', 'cols'), may hold values from -4 to 260
- out_weight: bfloat16 [256, 256], replicated, may hold values from -0.375 to 0.375
- unpatch: bfloat16 [256, 2048], replicated, may hold values from -0.375 to 0.375
- conv_out: bfloat16 [32, 288], replicated, may hold values from -0.375 to 0.375
Outputs:
- trunk_out: bfloat16 [32, 128, 2048], P(None, 'cols', 'rows')
The draws below stay inside these ranges and needn't reach their ends.
All inputs are finite; a program needn't handle non-finite values.
Results may differ from the reference program's by a relative error of at most 0.014.
Values may be sent and summed in bfloat16 or wider, within the bound.
A program may use at most 128 MiB of HBM per device.

```python
import jax
import jax.numpy as jnp
from jax import lax

C = 32
PATCH = 8
D = 256
HEADS = 8
HEAD_DIM = 32
ROWS_DEV = 128
COLS_DEV = 64
LENGTH = 2048
SLAB = 128
PROWS = 256
PCOLS = 16


def draw_pair_map(key, part):
    base_key = jax.random.fold_in(key, 23)
    map_shape = (C, SLAB, LENGTH)
    col_place = jnp.arange(SLAB) % COLS_DEV
    row_place = jnp.arange(LENGTH) % ROWS_DEV
    col_edge = jnp.logical_or(col_place == 0, col_place == COLS_DEV - 1)
    row_edge = jnp.logical_or(row_place == 0, row_place == ROWS_DEV - 1)
    corner = jnp.logical_and(col_edge[:, None], row_edge[None, :])[None, :, :]
    spread = jnp.clip(jax.random.normal(base_key, map_shape, jnp.float32), -6.0, 6.0)
    peak = jnp.where(spread >= 0.0, 1.0, -1.0) * (28.0 + 4.0 * jnp.minimum(jnp.abs(spread), 4.0))
    return jnp.where(corner, peak, spread).astype(jnp.bfloat16)


def draw_key_bias(key, part):
    base_key = jax.random.fold_in(key, 11)
    key_list = jax.random.split(base_key, 5)
    bias_shape = (PROWS, PCOLS, HEADS)
    pair_count = PCOLS * HEADS
    row_index = jnp.arange(PROWS)[:, None]
    background = jax.random.uniform(key_list[0], (PROWS, pair_count), jnp.float32, 0.0, 0.9)
    spike_row = jax.random.randint(key_list[4], (pair_count,), 0, PROWS)
    values = jnp.where(row_index == spike_row[None, :], 8.0, background)
    return values.reshape(bias_shape).astype(jnp.bfloat16)


def noise(key, dims, width, bound, dtype=jnp.bfloat16):
    entries = jax.random.normal(key, dims, jnp.float32) * width
    return jnp.minimum(jnp.maximum(entries, -bound), bound).astype(dtype)


def setup_inputs(seed: int = 0) -> dict:
    key_of = jax.random.split(jax.random.key(seed), 9)
    pair_map = draw_pair_map(jax.random.fold_in(key_of[8], 71), 0)
    conv_in = noise(key_of[1], (C, 9 * C), (9 * C) ** -0.5, 0.375)
    embed_weight = noise(key_of[2], (C * PATCH * PATCH, D), (C * PATCH * PATCH) ** -0.5, 0.125)
    qkv_weight = noise(key_of[3], (D, 3 * D), (D // 2) ** -0.5, 0.5)
    key_bias = draw_key_bias(jax.random.fold_in(key_of[8], 71), 0)
    out_weight = noise(key_of[5], (D, D), D ** -0.5, 0.375)
    unpatch = noise(key_of[6], (D, C * PATCH * PATCH), D ** -0.5, 0.375)
    conv_out = noise(key_of[7], (C, 9 * C), (9 * C) ** -0.5, 0.375)
    return dict(pair_map=pair_map, conv_in=conv_in, embed_weight=embed_weight, qkv_weight=qkv_weight, key_bias=key_bias, out_weight=out_weight, unpatch=unpatch, conv_out=conv_out)


epsilon = 1e-05

def convolve(source_map, weight):
    kernel = weight.astype(jnp.float32).reshape(C, 3, 3, C).transpose(0, 3, 1, 2)
    result = lax.conv_general_dilated(source_map.astype(jnp.float32)[None], kernel, (1, 1), ((1, 1), (1, 1)), dimension_numbers=('NCHW', 'OIHW', 'NCHW'), precision=lax.Precision.HIGHEST)
    return result[0]

def layer_norm(tokens):
    values = tokens.astype(jnp.float32)
    row_mean = lax.optimization_barrier(jnp.mean(values, axis=1, keepdims=True))
    centered = values - row_mean
    row_var = lax.optimization_barrier(jnp.mean(centered * centered, axis=1, keepdims=True))
    return (centered * lax.rsqrt(row_var + epsilon)).astype(jnp.bfloat16)

def attend(qkv_rows, bias_row):
    seq_length = qkv_rows.shape[0]
    block_rows = min(512, seq_length)
    queries = qkv_rows[:, :HEAD_DIM]
    key_rows = qkv_rows[:, HEAD_DIM:2 * HEAD_DIM]
    value_rows = qkv_rows[:, 2 * HEAD_DIM:]
    key_shift = bias_row.astype(jnp.float32)[None, :]
    score_scale = HEAD_DIM ** (-0.5)

    def one_block(query_block):
        scores = jnp.dot(query_block, key_rows.T, preferred_element_type=jnp.float32) * score_scale + key_shift
        row_peak = lax.optimization_barrier(jnp.max(scores, axis=1, keepdims=True))
        weights = jnp.exp(scores - row_peak)
        soft_weights = (weights / lax.optimization_barrier(jnp.sum(weights, axis=1, keepdims=True))).astype(jnp.bfloat16)
        return jnp.dot(soft_weights, value_rows, preferred_element_type=jnp.float32).astype(jnp.bfloat16)
    result = lax.map(one_block, queries.reshape(seq_length // block_rows, block_rows, HEAD_DIM))
    return result.reshape(seq_length, HEAD_DIM)

def attend_pair(pair_item):
    return attend(pair_item[0], pair_item[1])

def reference(pair_map, conv_in, embed_weight, qkv_weight, key_bias, out_weight, unpatch, conv_out):
    first_conv = convolve(pair_map, conv_in)
    mixed_map = (pair_map.astype(jnp.float32) + jax.nn.silu(first_conv)).astype(jnp.bfloat16)
    patches = mixed_map.reshape(C, PCOLS, PATCH, PROWS, PATCH).transpose(3, 1, 0, 2, 4).reshape(PROWS * PCOLS, C * PATCH * PATCH)
    tokens = jnp.dot(patches, embed_weight, preferred_element_type=jnp.float32).astype(jnp.bfloat16)
    normed = layer_norm(tokens)
    projected = jnp.dot(normed, qkv_weight, preferred_element_type=jnp.float32).astype(jnp.bfloat16)
    pair_items = projected.reshape(PROWS, PCOLS, 3, HEADS, HEAD_DIM).transpose(1, 3, 0, 2, 4).reshape(PCOLS * HEADS, PROWS, 3 * HEAD_DIM)
    biases = key_bias.transpose(1, 2, 0).reshape(PCOLS * HEADS, PROWS)
    attended = lax.map(attend_pair, (pair_items, biases))
    attended = attended.reshape(PCOLS, HEADS, PROWS, HEAD_DIM).transpose(2, 0, 1, 3).reshape(PROWS * PCOLS, D)
    updated = (tokens.astype(jnp.float32) + jnp.dot(attended, out_weight, preferred_element_type=jnp.float32)).astype(jnp.bfloat16)
    expanded = jnp.dot(updated, unpatch, preferred_element_type=jnp.float32)
    expanded = expanded.reshape(PROWS, PCOLS, C, PATCH, PATCH).transpose(2, 1, 3, 0, 4).reshape(C, SLAB, LENGTH)
    merged = (mixed_map.astype(jnp.float32) + expanded).astype(jnp.bfloat16)
    second_conv = convolve(merged, conv_out)
    return (merged.astype(jnp.float32) + second_conv).astype(jnp.bfloat16)
```

```python
import functools

import jax
import jax.numpy as jnp
from jax import lax
from jax.experimental import pallas as pl
from jax.experimental.pallas import tpu as pltpu
from jax.sharding import PartitionSpec as P

C = 32
PATCH = 8
D = 256
HEADS = 8
HEAD_DIM = 32
LANES = 128
EPSILON = 1e-05
F32 = jnp.float32
BF16 = jnp.bfloat16
MESH = pl.DeviceIdType.MESH
NT = (((1,), (1,)), ((), ()))
TOP = 8
VMEM_BYTES = 56 * 1024 * 1024


def dot(a, b):
    return jnp.dot(a, b, preferred_element_type=F32)


def dot_nt(a, b):
    return lax.dot_general(a, b, NT, preferred_element_type=F32)


def iota(shape, dim):
    return lax.broadcasted_iota(jnp.int32, shape, dim)


def trunk_kernel(
    R,
    NC,
    x_hbm,
    kb_hbm,
    cin_hbm,
    cout_hbm,
    embed_hbm,
    qkv_hbm,
    outw_hbm,
    unp_hbm,
    o_ref,
    x_v,
    kb_v,
    cin_v,
    cout_v,
    embed_v,
    qkv_v,
    outw_v,
    unp_v,
    tmap,
    mixed,
    edges,
    halo,
    edges2,
    halo2,
    wide,
    embed_i,
    unp_i,
    taps,
    sendk,
    recvk,
    sendq,
    recvq,
    sendb,
    recvb,
    sendo,
    recvo,
    x_sem,
    load_sem,
    halo_ss,
    halo_rs,
    col_ss,
    col_rs,
    h2_ss,
    h2_rs,
    k_ss,
    k_rs,
    q_ss,
    q_rs,
    b_ss,
    b_rs,
    o_ss,
    o_rs,
    met,
):
    row = lax.axis_index("rows")
    col = lax.axis_index("cols")
    NP = x_v.shape[1] // PATCH
    L = x_v.shape[2]
    PR = L // PATCH
    CJ = C * PATCH
    GH = D // LANES
    groups = NP * GH
    split = R // groups
    group_heads = LANES // HEAD_DIM
    my_heads = group_heads // split
    keys = R * PR
    bits = R.bit_length() - 1
    low = 2 ** (bits // 2)

    row_ok = {-1: row > 0, 1: row < R - 1}
    col_ok = {-1: col > 0, 0: col >= 0, 1: col < NC - 1}
    barrier = pltpu.get_barrier_semaphore()

    def partner(k):
        return row + (1 - 2 * lax.rem(row // 2**k, 2)) * 2**k

    flips = [partner(k) - row for k in range(bits)]

    def peer_at(d):
        peer = row
        for k in range(bits):
            if d // 2**k % 2:
                peer = peer + flips[k]
        return peer

    def greet(peer_row, peer_col):
        pl.semaphore_signal(
            barrier,
            inc=1,
            device_id={"rows": peer_row, "cols": peer_col},
            device_id_type=MESH,
        )

    lines = list(range(R - low, 0, -low)) + list(range(low - 1, 0, -1))
    for d in lines:
        greet(peer_at(d), col)
    expected = len(lines)
    for dr in (-1, 1):
        expected = expected + row_ok[dr].astype(jnp.int32)

        @pl.when(row_ok[dr])
        def _():
            greet(row + dr, col)

    for dc in (-1, 1):
        for dr in (-1, 0, 1):
            ok = col_ok[dc] if dr == 0 else jnp.logical_and(col_ok[dc], row_ok[dr])
            expected = expected + ok.astype(jnp.int32)

            @pl.when(ok)
            def _():
                greet(row + dr, col + dc)

    x_loads = [
        pltpu.make_async_copy(
            x_hbm.at[:, pl.ds(2 * PATCH * q, 2 * PATCH), :],
            x_v.at[:, pl.ds(2 * PATCH * q, 2 * PATCH), :],
            x_sem.at[q],
        )
        for q in range(NP // 2)
    ]
    for copy in x_loads:
        copy.start()
    loads = [
        pltpu.make_async_copy(src, dst, load_sem.at[n])
        for n, (src, dst) in enumerate(
            (
                (cin_hbm, cin_v),
                (embed_hbm, embed_v),
                (kb_hbm, kb_v),
                (qkv_hbm, qkv_v),
                (unp_hbm, unp_v),
                (cout_hbm, cout_v),
                (outw_hbm, outw_v),
            )
        )
    ]
    cin_load, embed_load, kb_load, qkv_load, unp_load, cout_load, outw_load = loads
    for copy in loads:
        copy.start()

    for q in range(NP // 2):
        x_loads[q].wait()
        pair = x_v[:, 2 * PATCH * q : 2 * PATCH * (q + 1), :].astype(F32)
        for s in range(2):
            block = pair[:, PATCH * s : PATCH * (s + 1), :].reshape(CJ, L)
            tmap[0, 1 + 2 * q + s, TOP : TOP + L, :] = block.T
    for p in range(NP):
        edges[0, p : p + 1, :] = tmap[0, p + 1, TOP + L - 1 : TOP + L, :]
        edges[1, p : p + 1, :] = tmap[0, p + 1, TOP : TOP + 1, :]

    pl.semaphore_wait(barrier, expected)

    def act_on(copy, act):
        if act == "start":
            copy.start()
        elif act == "send":
            copy.wait_send()
        else:
            copy.wait_recv()

    def col_copies(phase, act):
        place = pl.ds(TOP, L) if phase == 0 else pl.ds(0, L + 2 * TOP)
        for side, dc in ((0, 1), (1, -1)):
            copy = pltpu.make_async_remote_copy(
                src_ref=tmap.at[phase, NP if side == 0 else 1, place],
                dst_ref=tmap.at[phase, 0 if side == 0 else NP + 1, place],
                send_sem=col_ss.at[phase, side],
                recv_sem=col_rs.at[phase, side],
                device_id={"rows": row, "cols": col + (-dc if act == "recv" else dc)},
                device_id_type=MESH,
            )
            ok = col_ok[-dc] if act == "recv" else col_ok[dc]

            @pl.when(ok)
            def _():
                act_on(copy, act)

    def halo_copies(act):
        for way, dr in ((0, 1), (1, -1)):
            for slot in range(3):
                dc = slot - 1
                if act == "recv":
                    ok = jnp.logical_and(row_ok[-dr], col_ok[dc])
                    peer = {"rows": row - dr, "cols": col + dc}
                else:
                    ok = jnp.logical_and(row_ok[dr], col_ok[-dc])
                    peer = {"rows": row + dr, "cols": col - dc}
                copy = pltpu.make_async_remote_copy(
                    src_ref=edges.at[way],
                    dst_ref=halo.at[way, slot],
                    send_sem=halo_ss.at[way, slot],
                    recv_sem=halo_rs.at[way, slot],
                    device_id=peer,
                    device_id_type=MESH,
                )

                @pl.when(ok)
                def _():
                    act_on(copy, act)

    def edge_copies(act):
        for way, dr in ((0, 1), (1, -1)):
            copy = pltpu.make_async_remote_copy(
                src_ref=edges2.at[way],
                dst_ref=halo2.at[way],
                send_sem=h2_ss.at[way],
                recv_sem=h2_rs.at[way],
                device_id={"rows": row + (-dr if act == "recv" else dr), "cols": col},
                device_id_type=MESH,
            )

            @pl.when(row_ok[-dr] if act == "recv" else row_ok[dr])
            def _():
                act_on(copy, act)

    def exchange(act, source, target, send_sem, recv_sem):
        for d in range(R - 1, 0, -1):
            peer = peer_at(d)
            copy = pltpu.make_async_remote_copy(
                src_ref=source(peer),
                dst_ref=target.at[peer if act == "recv" else row],
                send_sem=send_sem.at[peer],
                recv_sem=recv_sem.at[peer if act == "recv" else row],
                device_id={"rows": peer, "cols": col},
                device_id_type=MESH,
            )
            act_on(copy, act)

    halo_copies("start")
    col_copies(0, "start")
    for d in range(1, low):
        pl.semaphore_signal(
            met, inc=1, device_id={"rows": peer_at(d), "cols": col}, device_id_type=MESH
        )

    for way, dr in ((0, -1), (1, 1)):
        for slot in range(3):
            missing = jnp.logical_not(jnp.logical_and(row_ok[dr], col_ok[slot - 1]))

            @pl.when(missing)
            def _():
                halo[way, slot] = jnp.zeros((NP, CJ), F32)

        @pl.when(jnp.logical_not(row_ok[dr]))
        def _():
            halo2[way] = jnp.zeros((2 * NP, CJ), F32)

    for side, dc in ((0, -1), (1, 1)):

        @pl.when(jnp.logical_not(col_ok[dc]))
        def _():
            tmap[0, side * (NP + 1), TOP : TOP + L, :] = jnp.zeros((L, CJ), F32)
            tmap[1, side * (NP + 1), :, :] = jnp.zeros((L + 2 * TOP, CJ), F32)

    tmap[0, :, 0:TOP, :] = jnp.zeros((NP + 2, TOP, CJ), F32)
    tmap[0, :, TOP + L : L + 2 * TOP, :] = jnp.zeros((NP + 2, TOP, CJ), F32)

    def banded(n, weight):
        spread = (iota((CJ, C), 0) // PATCH == iota((CJ, C), 1)).astype(F32).astype(BF16)
        wide_weight = dot(spread, weight).astype(BF16)
        shift = iota((CJ, CJ), 0) % PATCH - iota((CJ, CJ), 1) % PATCH
        ahead = iota((CJ, 9 * C), 1) - iota((CJ, 9 * C), 0) // PATCH
        for b in range(3):
            centre = jnp.zeros((CJ, CJ), F32)
            rim = jnp.zeros((CJ, CJ), F32)
            for a in range(3):
                pick = (ahead == (3 * a + b) * C).astype(F32).astype(BF16)
                full = dot_nt(pick, wide_weight)
                centre = jnp.where(shift == a - 1, full, centre)
                if a == 0:
                    rim = jnp.where(shift == PATCH - 1, full, rim)
                if a == 2:
                    rim = jnp.where(shift == 1 - PATCH, full, rim)
            taps[n, b, 0:CJ, :] = centre.astype(BF16)
            taps[n, b, CJ : 2 * CJ, :] = rim.astype(BF16)

    cin_load.wait()
    banded(0, cin_v[...])

    kb_load.wait()
    same = (iota((PR, PR), 0) == iota((PR, PR), 1)).astype(F32).astype(BF16)
    bias = dot_nt(same, kb_v[...].astype(F32).reshape(NP * HEADS, PR).astype(BF16))
    pad = jnp.zeros((PR, LANES - NP * HEADS), F32)
    sendk[...] = jnp.concatenate([bias, pad], axis=1).astype(BF16)

    embed_load.wait()
    for half in range(2):
        wide[half] = embed_v[:, half * LANES : (half + 1) * LANES].astype(F32)
    for i in range(PATCH):
        for half in range(2):
            embed_i[i, :, half * LANES : (half + 1) * LANES] = wide[
                half, pl.ds(i, CJ, stride=PATCH), :
            ].astype(BF16)

    lane_place = iota((1, 1, CJ), 2) % PATCH

    def rim_of(before, after):
        return jnp.where(lane_place == PATCH - 1, before, jnp.where(lane_place == 0, after, 0.0))

    def conv(phase, first, last):
        count = last - first
        total = None
        for b in range(3):
            cells = tmap[phase, first : last + 2, TOP - 1 + b : TOP - 1 + b + L, :]
            centre = cells[1 : count + 1].reshape(count * L, CJ).astype(BF16)
            rim = rim_of(cells[0:count], cells[2 : count + 2])
            rim = rim.reshape(count * L, CJ).astype(BF16)
            part = dot(centre, taps[phase, b, 0:CJ, :]) + dot(rim, taps[phase, b, CJ : 2 * CJ, :])
            total = part if total is None else total + part
        return total

    def silu(v):
        return v / (1.0 + jnp.exp(-v))

    col_copies(0, "recv")
    first = conv(0, 0, NP)
    base = tmap[0, 1 : NP + 1, TOP : TOP + L, :].reshape(NP * L, CJ)
    mix = (base + silu(first)).astype(BF16).astype(F32)
    for half in range(2):
        mixed[half] = mix[:, half * LANES : (half + 1) * LANES]
    first = first.reshape(NP, L, CJ)
    edge_conv = (first[:, 0, :], first[:, L - 1, :])

    if low > 1:
        pl.semaphore_wait(met, low - 1)
    k_source = lambda peer: sendk
    exchange("start", k_source, recvk, k_ss, k_rs)

    def embed(i, rows):
        return dot(rows.astype(BF16), embed_i[i])

    def normalise(tokens):
        mean = jnp.mean(tokens, axis=1, keepdims=True)
        centred = tokens - mean
        var = jnp.mean(centred * centred, axis=1, keepdims=True)
        return (centred * lax.rsqrt(var + EPSILON)).astype(BF16)

    parts = []
    for i in range(PATCH):
        cells = [mixed[half, pl.ds(i, NP * PR, stride=PATCH), :] for half in range(2)]
        parts.append(embed(i, jnp.concatenate(cells, axis=1)))
    middle = parts[1]
    for i in range(2, PATCH - 1):
        middle = middle + parts[i]
    inner = (middle + parts[0] + parts[PATCH - 1]).astype(BF16).astype(F32)
    qkv_load.wait()
    projected = dot(normalise(inner), qkv_v[...]).astype(BF16)
    for g in range(GH):
        for kind in range(3):
            start = kind * D + g * LANES
            part = projected[:, start : start + LANES].reshape(NP, PR, LANES)
            for p in range(NP):
                sendq[p * GH + g, :, kind * LANES : (kind + 1) * LANES] = part[p]
    q_source = lambda peer: sendq.at[peer // split]
    exchange("start", q_source, recvq, q_ss, q_rs)
    partial = (
        (middle + parts[PATCH - 1]).reshape(NP, PR, D)[:, 0, :],
        (middle + parts[0]).reshape(NP, PR, D)[:, PR - 1, :],
    )

    halo_copies("recv")
    edge_tokens = []
    for way, cell, tap in ((0, 0, 0), (1, L - 1, 2)):
        centre = halo[way, 1]
        before = jnp.concatenate([halo[way, 0, NP - 1 : NP, :], centre[0 : NP - 1]], axis=0)
        after = jnp.concatenate([centre[1:NP], halo[way, 2, 0:1, :]], axis=0)
        rim = rim_of(before[None], after[None])[0]
        extra = dot(centre.astype(BF16), taps[0, tap, 0:CJ, :])
        extra = extra + dot(rim.astype(BF16), taps[0, tap, CJ : 2 * CJ, :])
        fixed = (edges[1 - way] + silu(edge_conv[way] + extra)).astype(BF16).astype(F32)
        for half in range(2):
            mixed[half, pl.ds(cell, NP, stride=L), :] = fixed[:, half * LANES : (half + 1) * LANES]
        edge_token = partial[way] + embed(way * (PATCH - 1), fixed)
        edge_token = edge_token.astype(BF16).astype(F32)
        edge_tokens.append(edge_token)
        edges2[1 - way, 0:NP, :] = edge_token
        edges2[1 - way, NP : 2 * NP, :] = fixed
    edge_rows = dot(normalise(jnp.concatenate(edge_tokens, axis=0)), qkv_v[...])
    edge_rows = edge_rows.astype(BF16).astype(F32)
    for g in range(GH):
        for kind in range(3):
            start = kind * D + g * LANES
            for way in range(2):
                sendb[pl.ds(g * TOP + way * 3 + kind, NP, stride=GH * TOP), :] = edge_rows[
                    way * NP : (way + 1) * NP, start : start + LANES
                ]
    b_source = lambda peer: sendb.at[pl.ds(pl.multiple_of(peer // split * TOP, TOP), TOP)]
    exchange("start", b_source, recvb, b_ss, b_rs)
    edge_copies("start")
    recvq[row] = sendq[row // split]
    recvk[row] = sendk[...]
    recvb[row] = sendb[pl.ds(pl.multiple_of(row // split * TOP, TOP), TOP), :]

    place = iota((1, PR, 1), 1)
    tokens = jnp.where(
        place == 0,
        edge_tokens[0][:, None, :],
        jnp.where(place == PR - 1, edge_tokens[1][:, None, :], inner.reshape(NP, PR, D)),
    )

    unp_load.wait()
    for k in range(PATCH):
        block = unp_v[:, k * CJ : (k + 1) * CJ].astype(F32).T
        for half in range(2):
            wide[half, k * CJ : (k + 1) * CJ, :] = block[:, half * LANES : (half + 1) * LANES]
    for i in range(PATCH):
        for half in range(2):
            unp_i[i, :, half * LANES : (half + 1) * LANES] = wide[
                half, pl.ds(i, CJ, stride=PATCH), :
            ].astype(BF16)

    cout_load.wait()
    banded(1, cout_v[...])
    outw_load.wait()
    exchange("recv", k_source, recvk, k_ss, k_rs)
    first_head = lax.rem(row, split) * my_heads
    first_global = (row // split) * group_heads + first_head
    pick = (iota((16, LANES), 1) == iota((16, LANES), 0) + first_global).astype(F32).astype(BF16)
    key_shift = dot_nt(pick, recvk[...].reshape(keys, LANES))
    exchange("recv", q_source, recvq, q_ss, q_rs)
    exchange("recv", b_source, recvb, b_ss, b_rs)

    def received(kind):
        inside = recvq[:, :, kind * LANES : (kind + 1) * LANES].astype(F32)
        ends = [recvb[:, way * 3 + kind : way * 3 + kind + 1, :] for way in range(2)]
        whole = jnp.where(place == 0, ends[0], jnp.where(place == PR - 1, ends[1], inside))
        return whole.reshape(keys, LANES)

    queries = received(0)
    key_rows = received(1).astype(BF16)
    values = received(2)
    lane_head = iota((1, LANES), 1) // HEAD_DIM
    total = None
    for k in range(my_heads):
        mine = lane_head == first_head + k
        query = jnp.where(mine, queries, 0.0).astype(BF16)
        scores = dot_nt(query, key_rows) * (HEAD_DIM**-0.5) + key_shift[k : k + 1, :]
        weights = jnp.exp(scores - jnp.max(scores, axis=1, keepdims=True))
        soft = (weights * (1.0 / jnp.sum(weights, axis=1, keepdims=True))).astype(BF16)
        part = dot(soft, jnp.where(mine, values, 0.0).astype(BF16))
        total = part if total is None else total + part
    total = total.reshape(R, PR, LANES)
    sendo[:, 0:PR, :] = total.astype(BF16)
    above = jnp.concatenate([total[R - 1 : R], total[0 : R - 1]], axis=0)[:, PR - 1 : PR, :]
    below = jnp.concatenate([total[1:R], total[0:1]], axis=0)[:, 0:1, :]
    sendo[:, PR : 2 * PR, :] = jnp.where(
        place == 0, above, jnp.where(place == 1, below, 0.0)
    ).astype(BF16)
    o_source = lambda peer: sendo.at[peer]
    exchange("start", o_source, recvo, o_ss, o_rs)
    recvo[row] = sendo[row]
    edge_copies("recv")
    halo_copies("send")
    col_copies(0, "send")
    exchange("send", k_source, recvk, k_ss, k_rs)
    exchange("send", q_source, recvq, q_ss, q_rs)
    exchange("send", b_source, recvb, b_ss, b_rs)
    edge_copies("send")
    exchange("recv", o_source, recvo, o_ss, o_rs)

    back = recvo[...].reshape(NP, GH, split, 2 * PR, LANES)
    sides = []
    for g in range(GH):
        share = back[:, g, 0]
        for s in range(1, split):
            share = share + back[:, g, s]
        sides.append(share.reshape(NP * 2 * PR, LANES))
    attended = jnp.concatenate(sides, axis=1)
    change = dot(attended, outw_v[...]).reshape(NP, 2 * PR, D)
    updated = (tokens + change[:, 0:PR, :]).reshape(NP * PR, D).astype(BF16)
    for way, i in ((0, PATCH - 1), (1, 0)):
        outer = (halo2[way, 0:NP, :] + change[:, PR + way, :]).astype(BF16)
        outer = halo2[way, NP : 2 * NP, :] + dot_nt(outer, unp_i[i])
        outer = jnp.where(row_ok[2 * way - 1], outer, 0.0).astype(BF16).astype(F32)
        for p in range(NP):
            tmap[1, p + 1, way * (TOP + L) : way * (TOP + L) + TOP, :] = jnp.broadcast_to(
                outer[p : p + 1, :], (TOP, CJ)
            )
    for i in range(PATCH):
        expanded = dot_nt(updated, unp_i[i])
        for half in range(2):
            wide[half, pl.ds(i, NP * PR, stride=PATCH), :] = expanded[
                :, half * LANES : (half + 1) * LANES
            ]

    def merge(p):
        for half in range(2):
            cells = mixed[half, p * L : (p + 1) * L, :] + wide[half, p * L : (p + 1) * L, :]
            tmap[1, p + 1, TOP : TOP + L, half * LANES : (half + 1) * LANES] = cells.astype(
                BF16
            ).astype(F32)

    merge(0)
    merge(NP - 1)
    col_copies(1, "start")
    for p in range(1, NP - 1):
        merge(p)
    exchange("send", o_source, recvo, o_ss, o_rs)

    def finish(first, last):
        second = conv(1, first, last).reshape(last - first, L, CJ)
        return [
            (tmap[1, p + 1, TOP : TOP + L, :] + second[p - first]).T.reshape(C, PATCH, L)
            for p in range(first, last)
        ]

    def put(q, top, bottom):
        o_ref[:, 2 * PATCH * q : 2 * PATCH * (q + 1), :] = jnp.concatenate(
            [top, bottom], axis=1
        ).astype(BF16)

    inside = finish(1, NP - 1)
    for q in range(1, NP // 2 - 1):
        put(q, inside[2 * q - 1], inside[2 * q])
    col_copies(1, "recv")
    put(0, finish(0, 1)[0], inside[0])
    put(NP // 2 - 1, inside[NP - 3], finish(NP - 1, NP)[0])
    col_copies(1, "send")


def per_device(
    R, NC, pair_map, conv_in, embed_weight, qkv_weight, key_bias, out_weight, unpatch, conv_out
):
    NP = pair_map.shape[1] // PATCH
    L = pair_map.shape[2]
    PR = L // PATCH
    CJ = C * PATCH
    groups = NP * (D // LANES)
    hbm = pl.BlockSpec(memory_space=pltpu.HBM)
    dma = pltpu.SemaphoreType.DMA
    inputs = (
        pair_map,
        key_bias.transpose(1, 2, 0),
        conv_in,
        conv_out,
        embed_weight,
        qkv_weight,
        out_weight,
        unpatch,
    )
    return pl.pallas_call(
        functools.partial(trunk_kernel, R, NC),
        out_shape=pltpu.VMEM(pair_map.shape, BF16),
        in_specs=[hbm] * 8,
        out_specs=pl.BlockSpec(memory_space=pltpu.VMEM),
        scratch_shapes=[pltpu.VMEM(a.shape, BF16) for a in inputs]
        + [
            pltpu.VMEM((2, NP + 2, L + 2 * TOP, CJ), F32),
            pltpu.VMEM((2, NP * L, LANES), F32),
            pltpu.VMEM((2, NP, CJ), F32),
            pltpu.VMEM((2, 3, NP, CJ), F32),
            pltpu.VMEM((2, 2 * NP, CJ), F32),
            pltpu.VMEM((2, 2 * NP, CJ), F32),
            pltpu.VMEM((2, CJ * PATCH, LANES), F32),
            pltpu.VMEM((PATCH, CJ, D), BF16),
            pltpu.VMEM((PATCH, CJ, D), BF16),
            pltpu.VMEM((2, 3, 2 * CJ, CJ), BF16),
            pltpu.VMEM((PR, LANES), BF16),
            pltpu.VMEM((R, PR, LANES), BF16),
            pltpu.VMEM((groups, PR, 3 * LANES), BF16),
            pltpu.VMEM((R, PR, 3 * LANES), BF16),
            pltpu.VMEM((groups * TOP, LANES), F32),
            pltpu.VMEM((R, TOP, LANES), F32),
            pltpu.VMEM((R, 2 * PR, LANES), BF16),
            pltpu.VMEM((R, 2 * PR, LANES), BF16),
            dma((NP // 2,)),
            dma((7,)),
            dma((2, 3)),
            dma((2, 3)),
            dma((2, 2)),
            dma((2, 2)),
            dma((2,)),
            dma((2,)),
            dma((R,)),
            dma((R,)),
            dma((R,)),
            dma((R,)),
            dma((R,)),
            dma((R,)),
            dma((R,)),
            dma((R,)),
            pltpu.SemaphoreType.REGULAR,
        ],
        compiler_params=pltpu.CompilerParams(
            collective_id=0, has_side_effects=True, vmem_limit_bytes=VMEM_BYTES
        ),
    )(*inputs)


def solution(mesh):
    placed = (P(None, "cols", "rows"), P(), P(), P(), P("rows", "cols", None), P(), P(), P())
    return jax.shard_map(
        functools.partial(per_device, mesh.shape["rows"], mesh.shape["cols"]),
        mesh=mesh,
        in_specs=placed,
        out_specs=P(None, "cols", "rows"),
        check_vma=False,
    )
```

```python
import functools

import jax
import jax.numpy as jnp
from jax import lax
from jax.experimental import pallas as pl
from jax.experimental.pallas import tpu as pltpu
from jax.sharding import PartitionSpec as P

C = 32
PATCH = 8
D = 256
HEADS = 8
HEAD_DIM = 32
LANES = 128
EPSILON = 1e-05
F32 = jnp.float32
BF16 = jnp.bfloat16
MESH = pl.DeviceIdType.MESH
NT = (((1,), (1,)), ((), ()))
TOP = 8
VMEM_BYTES = 56 * 1024 * 1024


def dot(a, b):
    return jnp.dot(a, b, preferred_element_type=F32)


def dot_nt(a, b):
    return lax.dot_general(a, b, NT, preferred_element_type=F32)


def iota(shape, dim):
    return lax.broadcasted_iota(jnp.int32, shape, dim)


def trunk_kernel(
    R,
    NC,
    x_hbm,
    kb_hbm,
    cin_hbm,
    cout_hbm,
    embed_hbm,
    qkv_hbm,
    outw_hbm,
    unp_hbm,
    o_ref,
    x_v,
    kb_v,
    cin_v,
    cout_v,
    embed_v,
    qkv_v,
    outw_v,
    unp_v,
    tmap,
    mixed,
    edges,
    halo,
    edges2,
    halo2,
    wide,
    embed_i,
    unp_i,
    taps,
    sendk,
    recvk,
    sendq,
    recvq,
    sendo,
    recvo,
    x_sem,
    load_sem,
    halo_ss,
    halo_rs,
    col_ss,
    col_rs,
    h2_ss,
    h2_rs,
    k_ss,
    k_rs,
    q_ss,
    q_rs,
    o_ss,
    o_rs,
    met,
):
    row = lax.axis_index("rows")
    col = lax.axis_index("cols")
    NP = x_v.shape[1] // PATCH
    L = x_v.shape[2]
    PR = L // PATCH
    CJ = C * PATCH
    GH = D // LANES
    groups = NP * GH
    split = R // groups
    group_heads = LANES // HEAD_DIM
    my_heads = group_heads // split
    keys = R * PR
    bits = R.bit_length() - 1
    low = 2 ** (bits // 2)

    row_ok = {-1: row > 0, 1: row < R - 1}
    col_ok = {-1: col > 0, 0: col >= 0, 1: col < NC - 1}
    barrier = pltpu.get_barrier_semaphore()

    def partner(k):
        return row + (1 - 2 * lax.rem(row // 2**k, 2)) * 2**k

    flips = [partner(k) - row for k in range(bits)]

    def peer_at(d):
        peer = row
        for k in range(bits):
            if d // 2**k % 2:
                peer = peer + flips[k]
        return peer

    def greet(peer_row, peer_col):
        pl.semaphore_signal(
            barrier,
            inc=1,
            device_id={"rows": peer_row, "cols": peer_col},
            device_id_type=MESH,
        )

    lines = list(range(R - low, 0, -low)) + list(range(low - 1, 0, -1))
    for d in lines:
        greet(peer_at(d), col)
    expected = len(lines)
    for dr in (-1, 1):
        expected = expected + row_ok[dr].astype(jnp.int32)

        @pl.when(row_ok[dr])
        def _():
            greet(row + dr, col)

    for dc in (-1, 1):
        for dr in (-1, 0, 1):
            ok = col_ok[dc] if dr == 0 else jnp.logical_and(col_ok[dc], row_ok[dr])
            expected = expected + ok.astype(jnp.int32)

            @pl.when(ok)
            def _():
                greet(row + dr, col + dc)

    x_loads = [
        pltpu.make_async_copy(
            x_hbm.at[:, pl.ds(2 * PATCH * q, 2 * PATCH), :],
            x_v.at[:, pl.ds(2 * PATCH * q, 2 * PATCH), :],
            x_sem.at[q],
        )
        for q in range(NP // 2)
    ]
    loads = [
        pltpu.make_async_copy(src, dst, load_sem.at[n])
        for n, (src, dst) in enumerate(
            (
                (cin_hbm, cin_v),
                (embed_hbm, embed_v),
                (kb_hbm, kb_v),
                (qkv_hbm, qkv_v),
                (unp_hbm, unp_v),
                (cout_hbm, cout_v),
                (outw_hbm, outw_v),
            )
        )
    ]
    cin_load, embed_load, kb_load, qkv_load, unp_load, cout_load, outw_load = loads
    for copy in (cin_load, kb_load, *x_loads, embed_load, qkv_load, unp_load, cout_load, outw_load):
        copy.start()

    def banded(n, weight):
        spread = (iota((CJ, C), 0) // PATCH == iota((CJ, C), 1)).astype(F32).astype(BF16)
        wide_weight = dot(spread, weight).astype(BF16)
        shift = iota((CJ, CJ), 0) % PATCH - iota((CJ, CJ), 1) % PATCH
        ahead = iota((CJ, 9 * C), 1) - iota((CJ, 9 * C), 0) // PATCH
        for b in range(3):
            centre = jnp.zeros((CJ, CJ), F32)
            rim = jnp.zeros((CJ, CJ), F32)
            for a in range(3):
                pick = (ahead == (3 * a + b) * C).astype(F32).astype(BF16)
                full = dot_nt(pick, wide_weight)
                centre = jnp.where(shift == a - 1, full, centre)
                if a == 0:
                    rim = jnp.where(shift == PATCH - 1, full, rim)
                if a == 2:
                    rim = jnp.where(shift == 1 - PATCH, full, rim)
            taps[n, b, 0:CJ, :] = centre.astype(BF16)
            taps[n, b, CJ : 2 * CJ, :] = rim.astype(BF16)

    cin_load.wait()
    banded(0, cin_v[...])

    kb_load.wait()
    same = (iota((PR, PR), 0) == iota((PR, PR), 1)).astype(F32).astype(BF16)
    bias = dot_nt(same, kb_v[...].astype(F32).reshape(NP * HEADS, PR).astype(BF16))
    pad = jnp.zeros((PR, LANES - NP * HEADS), F32)
    sendk[...] = jnp.concatenate([bias, pad], axis=1).astype(BF16)

    for q in range(NP // 2):
        x_loads[q].wait()
        pair = x_v[:, 2 * PATCH * q : 2 * PATCH * (q + 1), :].astype(F32)
        for s in range(2):
            block = pair[:, PATCH * s : PATCH * (s + 1), :].reshape(CJ, L)
            tmap[0, 1 + 2 * q + s, TOP : TOP + L, :] = block.T
    for p in range(NP):
        edges[0, p : p + 1, :] = tmap[0, p + 1, TOP + L - 1 : TOP + L, :]
        edges[1, p : p + 1, :] = tmap[0, p + 1, TOP : TOP + 1, :]

    for way, dr in ((0, -1), (1, 1)):
        for slot in range(3):
            missing = jnp.logical_not(jnp.logical_and(row_ok[dr], col_ok[slot - 1]))

            @pl.when(missing)
            def _():
                halo[way, slot] = jnp.zeros((NP, CJ), F32)

        @pl.when(jnp.logical_not(row_ok[dr]))
        def _():
            halo2[way] = jnp.zeros((2 * NP, CJ), F32)

    for side, dc in ((0, -1), (1, 1)):

        @pl.when(jnp.logical_not(col_ok[dc]))
        def _():
            tmap[0, side * (NP + 1), TOP : TOP + L, :] = jnp.zeros((L, CJ), F32)
            tmap[1, side * (NP + 1), :, :] = jnp.zeros((L + 2 * TOP, CJ), F32)

    tmap[0, :, 0:TOP, :] = jnp.zeros((NP + 2, TOP, CJ), F32)
    tmap[0, :, TOP + L : L + 2 * TOP, :] = jnp.zeros((NP + 2, TOP, CJ), F32)

    pl.semaphore_wait(barrier, expected)

    for d in range(1, low):
        pl.semaphore_signal(
            met, inc=1, device_id={"rows": peer_at(d), "cols": col}, device_id_type=MESH
        )

    def act_on(copy, act):
        if act == "start":
            copy.start()
        elif act == "send":
            copy.wait_send()
        else:
            copy.wait_recv()

    def col_copies(phase, act):
        place = pl.ds(TOP, L) if phase == 0 else pl.ds(0, L + 2 * TOP)
        for side, dc in ((0, 1), (1, -1)):
            copy = pltpu.make_async_remote_copy(
                src_ref=tmap.at[phase, NP if side == 0 else 1, place],
                dst_ref=tmap.at[phase, 0 if side == 0 else NP + 1, place],
                send_sem=col_ss.at[phase, side],
                recv_sem=col_rs.at[phase, side],
                device_id={"rows": row, "cols": col + (-dc if act == "recv" else dc)},
                device_id_type=MESH,
            )
            ok = col_ok[-dc] if act == "recv" else col_ok[dc]

            @pl.when(ok)
            def _():
                act_on(copy, act)

    def halo_copies(act):
        for way, dr in ((0, 1), (1, -1)):
            for slot in range(3):
                dc = slot - 1
                if act == "recv":
                    ok = jnp.logical_and(row_ok[-dr], col_ok[dc])
                    peer = {"rows": row - dr, "cols": col + dc}
                else:
                    ok = jnp.logical_and(row_ok[dr], col_ok[-dc])
                    peer = {"rows": row + dr, "cols": col - dc}
                copy = pltpu.make_async_remote_copy(
                    src_ref=edges.at[way],
                    dst_ref=halo.at[way, slot],
                    send_sem=halo_ss.at[way, slot],
                    recv_sem=halo_rs.at[way, slot],
                    device_id=peer,
                    device_id_type=MESH,
                )

                @pl.when(ok)
                def _():
                    act_on(copy, act)

    def edge_copies(act):
        for way, dr in ((0, 1), (1, -1)):
            copy = pltpu.make_async_remote_copy(
                src_ref=edges2.at[way],
                dst_ref=halo2.at[way],
                send_sem=h2_ss.at[way],
                recv_sem=h2_rs.at[way],
                device_id={"rows": row + (-dr if act == "recv" else dr), "cols": col},
                device_id_type=MESH,
            )

            @pl.when(row_ok[-dr] if act == "recv" else row_ok[dr])
            def _():
                act_on(copy, act)

    def exchange(act, source, target, send_sem, recv_sem):
        for d in range(R - 1, 0, -1):
            peer = peer_at(d)
            copy = pltpu.make_async_remote_copy(
                src_ref=source(peer),
                dst_ref=target.at[peer if act == "recv" else row],
                send_sem=send_sem.at[peer],
                recv_sem=recv_sem.at[peer if act == "recv" else row],
                device_id={"rows": peer, "cols": col},
                device_id_type=MESH,
            )
            act_on(copy, act)

    halo_copies("start")
    col_copies(0, "start")
    lane_place = iota((1, 1, CJ), 2) % PATCH

    def rim_of(before, after):
        return jnp.where(lane_place == PATCH - 1, before, jnp.where(lane_place == 0, after, 0.0))

    def conv(phase, first, last):
        count = last - first
        total = None
        for b in range(3):
            cells = tmap[phase, first : last + 2, TOP - 1 + b : TOP - 1 + b + L, :]
            centre = cells[1 : count + 1].reshape(count * L, CJ).astype(BF16)
            rim = rim_of(cells[0:count], cells[2 : count + 2])
            rim = rim.reshape(count * L, CJ).astype(BF16)
            part = dot(centre, taps[phase, b, 0:CJ, :]) + dot(rim, taps[phase, b, CJ : 2 * CJ, :])
            total = part if total is None else total + part
        return total

    def silu(v):
        return v * (0.5 + 0.5 * jnp.tanh(0.5 * v))

    embed_load.wait()
    for half in range(2):
        wide[half] = embed_v[:, half * LANES : (half + 1) * LANES].astype(F32)
    for i in range(PATCH):
        for half in range(2):
            embed_i[i, :, half * LANES : (half + 1) * LANES] = wide[
                half, pl.ds(i, CJ, stride=PATCH), :
            ].astype(BF16)

    edge_conv = ([None] * NP, [None] * NP)

    def mix(start, stop):
        count = stop - start
        inner = conv(0, start, stop)
        base = tmap[0, start + 1 : stop + 1, TOP : TOP + L, :].reshape(count * L, CJ)
        cells = (base + silu(inner)).astype(BF16).astype(F32)
        for half in range(2):
            mixed[half, start * L : stop * L, :] = cells[:, half * LANES : (half + 1) * LANES]
        for p in range(start, stop):
            edge_conv[0][p] = inner[(p - start) * L : (p - start) * L + 1, :]
            edge_conv[1][p] = inner[(p - start + 1) * L - 1 : (p - start + 1) * L, :]

    mix(1, NP - 1)
    col_copies(0, "recv")
    if low > 1:
        pl.semaphore_wait(met, low - 1)
    k_source = lambda peer: sendk
    exchange("start", k_source, recvk, k_ss, k_rs)
    mix(0, 1)
    mix(NP - 1, NP)
    edge_conv = [jnp.concatenate(rows, axis=0) for rows in edge_conv]

    def embed(i, rows):
        return dot(rows.astype(BF16), embed_i[i])

    def normalise(tokens):
        mean = jnp.mean(tokens, axis=1, keepdims=True)
        centred = tokens - mean
        var = jnp.mean(centred * centred, axis=1, keepdims=True)
        return (centred * lax.rsqrt(var + EPSILON)).astype(BF16)

    parts = []
    for i in range(PATCH):
        cells = [mixed[half, pl.ds(i, NP * PR, stride=PATCH), :] for half in range(2)]
        parts.append(embed(i, jnp.concatenate(cells, axis=1)))
    middle = parts[1]
    for i in range(2, PATCH - 1):
        middle = middle + parts[i]
    inner = (middle + parts[0] + parts[PATCH - 1]).astype(BF16).astype(F32)
    partial = (
        (middle + parts[PATCH - 1]).reshape(NP, PR, D)[:, 0, :],
        (middle + parts[0]).reshape(NP, PR, D)[:, PR - 1, :],
    )

    halo_copies("recv")
    edge_tokens = []
    for way, cell, tap in ((0, 0, 0), (1, L - 1, 2)):
        centre = halo[way, 1]
        before = jnp.concatenate([halo[way, 0, NP - 1 : NP, :], centre[0 : NP - 1]], axis=0)
        after = jnp.concatenate([centre[1:NP], halo[way, 2, 0:1, :]], axis=0)
        rim = rim_of(before[None], after[None])[0]
        extra = dot(centre.astype(BF16), taps[0, tap, 0:CJ, :])
        extra = extra + dot(rim.astype(BF16), taps[0, tap, CJ : 2 * CJ, :])
        fixed = (edges[1 - way] + silu(edge_conv[way] + extra)).astype(BF16).astype(F32)
        for half in range(2):
            mixed[half, pl.ds(cell, NP, stride=L), :] = fixed[:, half * LANES : (half + 1) * LANES]
        edge_token = partial[way] + embed(way * (PATCH - 1), fixed)
        edge_token = edge_token.astype(BF16).astype(F32)
        edge_tokens.append(edge_token)
        edges2[1 - way, 0:NP, :] = edge_token
        edges2[1 - way, NP : 2 * NP, :] = fixed
    place = iota((1, PR, 1), 1)
    tokens = jnp.where(
        place == 0,
        edge_tokens[0][:, None, :],
        jnp.where(place == PR - 1, edge_tokens[1][:, None, :], inner.reshape(NP, PR, D)),
    )

    qkv_load.wait()
    projected = dot(normalise(tokens.reshape(NP * PR, D)), qkv_v[...]).astype(BF16)
    for g in range(GH):
        for kind in range(3):
            start = kind * D + g * LANES
            part = projected[:, start : start + LANES].reshape(NP, PR, LANES)
            for p in range(NP):
                sendq[p * GH + g, :, kind * LANES : (kind + 1) * LANES] = part[p]
    q_source = lambda peer: sendq.at[peer // split]
    exchange("start", q_source, recvq, q_ss, q_rs)
    edge_copies("start")
    recvq[row] = sendq[row // split]
    recvk[row] = sendk[...]

    unp_load.wait()
    for k in range(PATCH):
        block = unp_v[:, k * CJ : (k + 1) * CJ].astype(F32).T
        for half in range(2):
            wide[half, k * CJ : (k + 1) * CJ, :] = block[:, half * LANES : (half + 1) * LANES]
    for i in range(PATCH):
        for half in range(2):
            unp_i[i, :, half * LANES : (half + 1) * LANES] = wide[
                half, pl.ds(i, CJ, stride=PATCH), :
            ].astype(BF16)

    cout_load.wait()
    banded(1, cout_v[...])
    outw_load.wait()
    exchange("recv", k_source, recvk, k_ss, k_rs)
    first_head = lax.rem(row, split) * my_heads
    first_global = (row // split) * group_heads + first_head
    pick = (iota((16, LANES), 1) == iota((16, LANES), 0) + first_global).astype(F32).astype(BF16)
    key_shift = dot_nt(pick, recvk[...].reshape(keys, LANES))
    exchange("recv", q_source, recvq, q_ss, q_rs)

    queries = recvq[:, :, 0:LANES].astype(F32).reshape(keys, LANES)
    key_rows = recvq[:, :, LANES : 2 * LANES].reshape(keys, LANES)
    values = recvq[:, :, 2 * LANES : 3 * LANES].astype(F32).reshape(keys, LANES)
    lane_head = iota((1, LANES), 1) // HEAD_DIM
    total = None
    for k in range(my_heads):
        mine = lane_head == first_head + k
        query = jnp.where(mine, queries, 0.0).astype(BF16)
        scores = dot_nt(query, key_rows) * (HEAD_DIM**-0.5) + key_shift[k : k + 1, :]
        weights = jnp.exp(scores - jnp.max(scores, axis=1, keepdims=True))
        soft = (weights * (1.0 / jnp.sum(weights, axis=1, keepdims=True))).astype(BF16)
        part = dot(soft, jnp.where(mine, values, 0.0).astype(BF16))
        total = part if total is None else total + part
    total = total.reshape(R, PR, LANES)
    sendo[:, 0:PR, :] = total.astype(BF16)
    above = jnp.concatenate([total[R - 1 : R], total[0 : R - 1]], axis=0)[:, PR - 1 : PR, :]
    below = jnp.concatenate([total[1:R], total[0:1]], axis=0)[:, 0:1, :]
    sendo[:, PR : 2 * PR, :] = jnp.where(
        place == 0, above, jnp.where(place == 1, below, 0.0)
    ).astype(BF16)
    o_source = lambda peer: sendo.at[peer]
    exchange("start", o_source, recvo, o_ss, o_rs)
    recvo[row] = sendo[row]
    edge_copies("recv")
    halo_copies("send")
    col_copies(0, "send")
    exchange("send", k_source, recvk, k_ss, k_rs)
    exchange("send", q_source, recvq, q_ss, q_rs)
    edge_copies("send")
    exchange("recv", o_source, recvo, o_ss, o_rs)

    back = recvo[...].reshape(NP, GH, split, 2 * PR, LANES)
    sides = []
    for g in range(GH):
        share = back[:, g, 0]
        for s in range(1, split):
            share = share + back[:, g, s]
        sides.append(share.reshape(NP * 2 * PR, LANES))
    attended = jnp.concatenate(sides, axis=1)
    change = dot(attended, outw_v[...]).reshape(NP, 2 * PR, D)
    updated = (tokens + change[:, 0:PR, :]).reshape(NP * PR, D).astype(BF16)
    for way, i in ((0, PATCH - 1), (1, 0)):
        outer = (halo2[way, 0:NP, :] + change[:, PR + way, :]).astype(BF16)
        outer = halo2[way, NP : 2 * NP, :] + dot_nt(outer, unp_i[i])
        outer = jnp.where(row_ok[2 * way - 1], outer, 0.0).astype(BF16).astype(F32)
        for p in range(NP):
            tmap[1, p + 1, way * (TOP + L) : way * (TOP + L) + TOP, :] = jnp.broadcast_to(
                outer[p : p + 1, :], (TOP, CJ)
            )
    for i in range(PATCH):
        expanded = dot_nt(updated, unp_i[i])
        for half in range(2):
            wide[half, pl.ds(i, NP * PR, stride=PATCH), :] = expanded[
                :, half * LANES : (half + 1) * LANES
            ]

    def merge(p):
        for half in range(2):
            cells = mixed[half, p * L : (p + 1) * L, :] + wide[half, p * L : (p + 1) * L, :]
            tmap[1, p + 1, TOP : TOP + L, half * LANES : (half + 1) * LANES] = cells.astype(
                BF16
            ).astype(F32)

    merge(0)
    merge(NP - 1)
    col_copies(1, "start")
    for p in range(1, NP - 1):
        merge(p)
    exchange("send", o_source, recvo, o_ss, o_rs)

    def finish(first, last):
        second = conv(1, first, last).reshape(last - first, L, CJ)
        return [
            (tmap[1, p + 1, TOP : TOP + L, :] + second[p - first]).T.reshape(C, PATCH, L)
            for p in range(first, last)
        ]

    def put(q, top, bottom):
        o_ref[:, 2 * PATCH * q : 2 * PATCH * (q + 1), :] = jnp.concatenate(
            [top, bottom], axis=1
        ).astype(BF16)

    inside = finish(1, NP - 1)
    for q in range(1, NP // 2 - 1):
        put(q, inside[2 * q - 1], inside[2 * q])
    col_copies(1, "recv")
    put(0, finish(0, 1)[0], inside[0])
    put(NP // 2 - 1, inside[NP - 3], finish(NP - 1, NP)[0])
    col_copies(1, "send")


def per_device(
    R, NC, pair_map, conv_in, embed_weight, qkv_weight, key_bias, out_weight, unpatch, conv_out
):
    NP = pair_map.shape[1] // PATCH
    L = pair_map.shape[2]
    PR = L // PATCH
    CJ = C * PATCH
    groups = NP * (D // LANES)
    hbm = pl.BlockSpec(memory_space=pltpu.HBM)
    dma = pltpu.SemaphoreType.DMA
    inputs = (
        pair_map,
        key_bias.transpose(1, 2, 0),
        conv_in,
        conv_out,
        embed_weight,
        qkv_weight,
        out_weight,
        unpatch,
    )
    return pl.pallas_call(
        functools.partial(trunk_kernel, R, NC),
        out_shape=pltpu.VMEM(pair_map.shape, BF16),
        in_specs=[hbm] * 8,
        out_specs=pl.BlockSpec(memory_space=pltpu.VMEM),
        scratch_shapes=[pltpu.VMEM(a.shape, BF16) for a in inputs]
        + [
            pltpu.VMEM((2, NP + 2, L + 2 * TOP, CJ), F32),
            pltpu.VMEM((2, NP * L, LANES), F32),
            pltpu.VMEM((2, NP, CJ), F32),
            pltpu.VMEM((2, 3, NP, CJ), F32),
            pltpu.VMEM((2, 2 * NP, CJ), F32),
            pltpu.VMEM((2, 2 * NP, CJ), F32),
            pltpu.VMEM((2, CJ * PATCH, LANES), F32),
            pltpu.VMEM((PATCH, CJ, D), BF16),
            pltpu.VMEM((PATCH, CJ, D), BF16),
            pltpu.VMEM((2, 3, 2 * CJ, CJ), BF16),
            pltpu.VMEM((PR, LANES), BF16),
            pltpu.VMEM((R, PR, LANES), BF16),
            pltpu.VMEM((groups, PR, 3 * LANES), BF16),
            pltpu.VMEM((R, PR, 3 * LANES), BF16),
            pltpu.VMEM((R, 2 * PR, LANES), BF16),
            pltpu.VMEM((R, 2 * PR, LANES), BF16),
            dma((NP // 2,)),
            dma((7,)),
            dma((2, 3)),
            dma((2, 3)),
            dma((2, 2)),
            dma((2, 2)),
            dma((2,)),
            dma((2,)),
            dma((R,)),
            dma((R,)),
            dma((R,)),
            dma((R,)),
            dma((R,)),
            dma((R,)),
            pltpu.SemaphoreType.REGULAR,
        ],
        compiler_params=pltpu.CompilerParams(
            collective_id=0, has_side_effects=True, vmem_limit_bytes=VMEM_BYTES
        ),
    )(*inputs)


def solution(mesh):
    placed = (P(None, "cols", "rows"), P(), P(), P(), P("rows", "cols", None), P(), P(), P())
    return jax.shard_map(
        functools.partial(per_device, mesh.shape["rows"], mesh.shape["cols"]),
        mesh=mesh,
        in_specs=placed,
        out_specs=P(None, "cols", "rows"),
        check_vma=False,
    )
```

```python
import functools

import jax
import jax.numpy as jnp
from jax import lax
from jax.experimental import pallas as pl
from jax.experimental.pallas import tpu as pltpu
from jax.sharding import PartitionSpec as P

C = 32
PATCH = 8
D = 256
HEADS = 8
HEAD_DIM = 32
LANES = 128
EPSILON = 1e-05
F32 = jnp.float32
BF16 = jnp.bfloat16
MESH = pl.DeviceIdType.MESH
NT = (((1,), (1,)), ((), ()))
TOP = 8
VMEM_BYTES = 56 * 1024 * 1024


def dot(a, b):
    return jnp.dot(a, b, preferred_element_type=F32)


def dot_nt(a, b):
    return lax.dot_general(a, b, NT, preferred_element_type=F32)


def iota(shape, dim):
    return lax.broadcasted_iota(jnp.int32, shape, dim)


def trunk_kernel(
    R,
    NC,
    x_hbm,
    kb_hbm,
    cin_hbm,
    cout_hbm,
    embed_hbm,
    qkv_hbm,
    outw_hbm,
    unp_hbm,
    o_ref,
    x_v,
    kb_v,
    cin_v,
    cout_v,
    embed_v,
    qkv_v,
    outw_v,
    unp_v,
    tmap,
    mixed,
    edges,
    halo,
    edges2,
    halo2,
    wide,
    embed_i,
    unp_i,
    taps,
    sendk,
    recvk,
    sendq,
    recvq,
    sendo,
    recvo,
    x_sem,
    load_sem,
    halo_ss,
    halo_rs,
    col_ss,
    col_rs,
    h2_ss,
    h2_rs,
    k_ss,
    k_rs,
    q_ss,
    q_rs,
    o_ss,
    o_rs,
    met,
):
    row = lax.axis_index("rows")
    col = lax.axis_index("cols")
    NP = x_v.shape[1] // PATCH
    L = x_v.shape[2]
    PR = L // PATCH
    CJ = C * PATCH
    GH = D // LANES
    groups = NP * GH
    split = R // groups
    group_heads = LANES // HEAD_DIM
    my_heads = group_heads // split
    keys = R * PR
    bits = R.bit_length() - 1
    low = 2 ** (bits // 2)

    row_ok = {-1: row > 0, 1: row < R - 1}
    col_ok = {-1: col > 0, 0: col >= 0, 1: col < NC - 1}
    barrier = pltpu.get_barrier_semaphore()

    def partner(k):
        return row + (1 - 2 * lax.rem(row // 2**k, 2)) * 2**k

    flips = [partner(k) - row for k in range(bits)]

    def peer_at(d):
        peer = row
        for k in range(bits):
            if d // 2**k % 2:
                peer = peer + flips[k]
        return peer

    def greet(peer_row, peer_col):
        pl.semaphore_signal(
            barrier,
            inc=1,
            device_id={"rows": peer_row, "cols": peer_col},
            device_id_type=MESH,
        )

    lines = list(range(R - low, 0, -low)) + list(range(low - 1, 0, -1))
    for d in lines:
        greet(peer_at(d), col)
    expected = len(lines)
    for dr in (-1, 1):
        expected = expected + row_ok[dr].astype(jnp.int32)

        @pl.when(row_ok[dr])
        def _():
            greet(row + dr, col)

    for dc in (-1, 1):
        for dr in (-1, 0, 1):
            ok = col_ok[dc] if dr == 0 else jnp.logical_and(col_ok[dc], row_ok[dr])
            expected = expected + ok.astype(jnp.int32)

            @pl.when(ok)
            def _():
                greet(row + dr, col + dc)

    x_loads = [
        pltpu.make_async_copy(
            x_hbm.at[:, pl.ds(2 * PATCH * q, 2 * PATCH), :],
            x_v.at[:, pl.ds(2 * PATCH * q, 2 * PATCH), :],
            x_sem.at[q],
        )
        for q in range(NP // 2)
    ]
    loads = [
        pltpu.make_async_copy(src, dst, load_sem.at[n])
        for n, (src, dst) in enumerate(
            (
                (cin_hbm, cin_v),
                (embed_hbm, embed_v),
                (kb_hbm, kb_v),
                (qkv_hbm, qkv_v),
                (unp_hbm, unp_v),
                (cout_hbm, cout_v),
                (outw_hbm, outw_v),
            )
        )
    ]
    cin_load, embed_load, kb_load, qkv_load, unp_load, cout_load, outw_load = loads
    for copy in (cin_load, kb_load, *x_loads, embed_load, qkv_load, unp_load, cout_load, outw_load):
        copy.start()

    def banded(n, weight):
        spread = (iota((CJ, C), 0) // PATCH == iota((CJ, C), 1)).astype(F32).astype(BF16)
        wide_weight = dot(spread, weight).astype(BF16)
        shift = iota((CJ, CJ), 0) % PATCH - iota((CJ, CJ), 1) % PATCH
        ahead = iota((CJ, 9 * C), 1) - iota((CJ, 9 * C), 0) // PATCH
        for b in range(3):
            centre = jnp.zeros((CJ, CJ), F32)
            rim = jnp.zeros((CJ, CJ), F32)
            for a in range(3):
                start = (3 * a + b) * C
                lanes = slice(0, CJ) if start < CJ else slice(CJ, 9 * C)
                pick = (ahead[:, lanes] == start).astype(F32).astype(BF16)
                full = dot_nt(pick, wide_weight[:, lanes])
                centre = jnp.where(shift == a - 1, full, centre)
                if a == 0:
                    rim = jnp.where(shift == PATCH - 1, full, rim)
                if a == 2:
                    rim = jnp.where(shift == 1 - PATCH, full, rim)
            taps[n, b, 0:CJ, :] = centre.astype(BF16)
            taps[n, b, CJ : 2 * CJ, :] = rim.astype(BF16)

    cin_load.wait()
    banded(0, cin_v[...])

    kb_load.wait()
    same = (iota((PR, PR), 0) == iota((PR, PR), 1)).astype(F32).astype(BF16)
    bias = dot_nt(same, kb_v[...].astype(F32).reshape(NP * HEADS, PR).astype(BF16))
    pad = jnp.zeros((PR, LANES - NP * HEADS), F32)
    sendk[...] = jnp.concatenate([bias, pad], axis=1).astype(BF16)

    for q in range(NP // 2):
        x_loads[q].wait()
        pair = x_v[:, 2 * PATCH * q : 2 * PATCH * (q + 1), :].astype(F32)
        for s in range(2):
            block = pair[:, PATCH * s : PATCH * (s + 1), :].reshape(CJ, L)
            tmap[0, 1 + 2 * q + s, TOP : TOP + L, :] = block.T
    for p in range(NP):
        edges[0, p : p + 1, :] = tmap[0, p + 1, TOP + L - 1 : TOP + L, :]
        edges[1, p : p + 1, :] = tmap[0, p + 1, TOP : TOP + 1, :]

    for way, dr in ((0, -1), (1, 1)):
        for slot in range(3):
            missing = jnp.logical_not(jnp.logical_and(row_ok[dr], col_ok[slot - 1]))

            @pl.when(missing)
            def _():
                halo[way, slot] = jnp.zeros((NP, CJ), F32)

        @pl.when(jnp.logical_not(row_ok[dr]))
        def _():
            halo2[way] = jnp.zeros((2 * NP, CJ), F32)

    for side, dc in ((0, -1), (1, 1)):

        @pl.when(jnp.logical_not(col_ok[dc]))
        def _():
            tmap[0, side * (NP + 1), TOP : TOP + L, :] = jnp.zeros((L, CJ), F32)
            tmap[1, side * (NP + 1), :, :] = jnp.zeros((L + 2 * TOP, CJ), F32)

    tmap[0, :, 0:TOP, :] = jnp.zeros((NP + 2, TOP, CJ), F32)
    tmap[0, :, TOP + L : L + 2 * TOP, :] = jnp.zeros((NP + 2, TOP, CJ), F32)

    pl.semaphore_wait(barrier, expected)

    for d in range(1, low):
        pl.semaphore_signal(
            met, inc=1, device_id={"rows": peer_at(d), "cols": col}, device_id_type=MESH
        )

    def act_on(copy, act):
        if act == "start":
            copy.start()
        elif act == "send":
            copy.wait_send()
        else:
            copy.wait_recv()

    def col_copies(phase, act):
        place = pl.ds(TOP, L) if phase == 0 else pl.ds(0, L + 2 * TOP)
        for side, dc in ((0, 1), (1, -1)):
            copy = pltpu.make_async_remote_copy(
                src_ref=tmap.at[phase, NP if side == 0 else 1, place],
                dst_ref=tmap.at[phase, 0 if side == 0 else NP + 1, place],
                send_sem=col_ss.at[phase, side],
                recv_sem=col_rs.at[phase, side],
                device_id={"rows": row, "cols": col + (-dc if act == "recv" else dc)},
                device_id_type=MESH,
            )
            ok = col_ok[-dc] if act == "recv" else col_ok[dc]

            @pl.when(ok)
            def _():
                act_on(copy, act)

    def halo_copies(act):
        for way, dr in ((0, 1), (1, -1)):
            for slot in range(3):
                dc = slot - 1
                if act == "recv":
                    ok = jnp.logical_and(row_ok[-dr], col_ok[dc])
                    peer = {"rows": row - dr, "cols": col + dc}
                else:
                    ok = jnp.logical_and(row_ok[dr], col_ok[-dc])
                    peer = {"rows": row + dr, "cols": col - dc}
                copy = pltpu.make_async_remote_copy(
                    src_ref=edges.at[way],
                    dst_ref=halo.at[way, slot],
                    send_sem=halo_ss.at[way, slot],
                    recv_sem=halo_rs.at[way, slot],
                    device_id=peer,
                    device_id_type=MESH,
                )

                @pl.when(ok)
                def _():
                    act_on(copy, act)

    def edge_copies(act):
        for way, dr in ((0, 1), (1, -1)):
            copy = pltpu.make_async_remote_copy(
                src_ref=edges2.at[way],
                dst_ref=halo2.at[way],
                send_sem=h2_ss.at[way],
                recv_sem=h2_rs.at[way],
                device_id={"rows": row + (-dr if act == "recv" else dr), "cols": col},
                device_id_type=MESH,
            )

            @pl.when(row_ok[-dr] if act == "recv" else row_ok[dr])
            def _():
                act_on(copy, act)

    def exchange(act, source, target, send_sem, recv_sem):
        for d in range(R - 1, 0, -1):
            peer = peer_at(d)
            copy = pltpu.make_async_remote_copy(
                src_ref=source(peer),
                dst_ref=target.at[peer if act == "recv" else row],
                send_sem=send_sem.at[peer],
                recv_sem=recv_sem.at[peer if act == "recv" else row],
                device_id={"rows": peer, "cols": col},
                device_id_type=MESH,
            )
            act_on(copy, act)

    halo_copies("start")
    col_copies(0, "start")
    lane_place = iota((1, 1, CJ), 2) % PATCH

    def rim_of(before, after):
        return jnp.where(lane_place == PATCH - 1, before, jnp.where(lane_place == 0, after, 0.0))

    def conv(phase, blocks):
        count = len(blocks)
        total = None
        for b in range(3):
            rows = slice(TOP - 1 + b, TOP - 1 + b + L)
            centre, before, after = (
                jnp.concatenate([tmap[phase, p + d : p + d + 1, rows, :] for p in blocks], axis=0)
                for d in (1, 0, 2)
            )
            centre = centre.reshape(count * L, CJ).astype(BF16)
            rim = rim_of(before, after).reshape(count * L, CJ).astype(BF16)
            part = dot(centre, taps[phase, b, 0:CJ, :]) + dot(rim, taps[phase, b, CJ : 2 * CJ, :])
            total = part if total is None else total + part
        return total.reshape(count, L, CJ)

    def silu(v):
        return v * (0.5 + 0.5 * jnp.tanh(0.5 * v))

    embed_load.wait()
    for half in range(2):
        wide[half] = embed_v[:, half * LANES : (half + 1) * LANES].astype(F32)
    for i in range(PATCH):
        for half in range(2):
            embed_i[i, :, half * LANES : (half + 1) * LANES] = wide[
                half, pl.ds(i, CJ, stride=PATCH), :
            ].astype(BF16)

    edge_conv = ([None] * NP, [None] * NP)

    middle_blocks = list(range(1, NP - 1))
    outer_blocks = [0, NP - 1]

    def mix(blocks):
        inner = conv(0, blocks)
        for n, p in enumerate(blocks):
            base = tmap[0, p + 1, TOP : TOP + L, :]
            cells = (base + silu(inner[n])).astype(BF16).astype(F32)
            for half in range(2):
                mixed[half, p * L : (p + 1) * L, :] = cells[:, half * LANES : (half + 1) * LANES]
            edge_conv[0][p] = inner[n, 0:1, :]
            edge_conv[1][p] = inner[n, L - 1 : L, :]

    mix(middle_blocks)
    col_copies(0, "recv")
    if low > 1:
        pl.semaphore_wait(met, low - 1)
    k_source = lambda peer: sendk
    exchange("start", k_source, recvk, k_ss, k_rs)
    mix(outer_blocks)
    edge_conv = [jnp.concatenate(rows, axis=0) for rows in edge_conv]

    def embed(i, rows):
        return dot(rows.astype(BF16), embed_i[i])

    def normalise(tokens):
        mean = jnp.mean(tokens, axis=1, keepdims=True)
        centred = tokens - mean
        var = jnp.mean(centred * centred, axis=1, keepdims=True)
        return (centred * lax.rsqrt(var + EPSILON)).astype(BF16)

    parts = []
    for i in range(PATCH):
        cells = [mixed[half, pl.ds(i, NP * PR, stride=PATCH), :] for half in range(2)]
        parts.append(embed(i, jnp.concatenate(cells, axis=1)))
    middle = parts[1]
    for i in range(2, PATCH - 1):
        middle = middle + parts[i]
    inner = (middle + parts[0] + parts[PATCH - 1]).astype(BF16).astype(F32)
    partial = (
        (middle + parts[PATCH - 1]).reshape(NP, PR, D)[:, 0, :],
        (middle + parts[0]).reshape(NP, PR, D)[:, PR - 1, :],
    )

    halo_copies("recv")
    edge_tokens = []
    for way, cell, tap in ((0, 0, 0), (1, L - 1, 2)):
        centre = halo[way, 1]
        before = jnp.concatenate([halo[way, 0, NP - 1 : NP, :], centre[0 : NP - 1]], axis=0)
        after = jnp.concatenate([centre[1:NP], halo[way, 2, 0:1, :]], axis=0)
        rim = rim_of(before[None], after[None])[0]
        extra = dot(centre.astype(BF16), taps[0, tap, 0:CJ, :])
        extra = extra + dot(rim.astype(BF16), taps[0, tap, CJ : 2 * CJ, :])
        fixed = (edges[1 - way] + silu(edge_conv[way] + extra)).astype(BF16).astype(F32)
        for half in range(2):
            mixed[half, pl.ds(cell, NP, stride=L), :] = fixed[:, half * LANES : (half + 1) * LANES]
        edge_token = partial[way] + embed(way * (PATCH - 1), fixed)
        edge_token = edge_token.astype(BF16).astype(F32)
        edge_tokens.append(edge_token)
        edges2[1 - way, 0:NP, :] = edge_token
        edges2[1 - way, NP : 2 * NP, :] = fixed
    place = iota((1, PR, 1), 1)
    tokens = jnp.where(
        place == 0,
        edge_tokens[0][:, None, :],
        jnp.where(place == PR - 1, edge_tokens[1][:, None, :], inner.reshape(NP, PR, D)),
    )

    qkv_load.wait()
    projected = dot(normalise(tokens.reshape(NP * PR, D)), qkv_v[...]).astype(BF16)
    for g in range(GH):
        for kind in range(3):
            start = kind * D + g * LANES
            part = projected[:, start : start + LANES].reshape(NP, PR, LANES)
            for p in range(NP):
                sendq[p * GH + g, :, kind * LANES : (kind + 1) * LANES] = part[p]
    q_source = lambda peer: sendq.at[peer // split]
    exchange("start", q_source, recvq, q_ss, q_rs)
    edge_copies("start")
    recvq[row] = sendq[row // split]
    recvk[row] = sendk[...]

    unp_load.wait()
    for k in range(PATCH):
        block = unp_v[:, k * CJ : (k + 1) * CJ].astype(F32).T
        for half in range(2):
            wide[half, k * CJ : (k + 1) * CJ, :] = block[:, half * LANES : (half + 1) * LANES]
    for i in range(PATCH):
        for half in range(2):
            unp_i[i, :, half * LANES : (half + 1) * LANES] = wide[
                half, pl.ds(i, CJ, stride=PATCH), :
            ].astype(BF16)

    cout_load.wait()
    banded(1, cout_v[...])
    outw_load.wait()
    exchange("recv", k_source, recvk, k_ss, k_rs)
    first_head = lax.rem(row, split) * my_heads
    first_global = (row // split) * group_heads + first_head
    pick = (iota((16, LANES), 1) == iota((16, LANES), 0) + first_global).astype(F32).astype(BF16)
    key_shift = dot_nt(pick, recvk[...].reshape(keys, LANES))
    exchange("recv", q_source, recvq, q_ss, q_rs)

    queries = recvq[:, :, 0:LANES].astype(F32).reshape(keys, LANES)
    key_rows = recvq[:, :, LANES : 2 * LANES].reshape(keys, LANES)
    values = recvq[:, :, 2 * LANES : 3 * LANES].astype(F32).reshape(keys, LANES)
    lane_head = iota((1, LANES), 1) // HEAD_DIM
    total = None
    for k in range(my_heads):
        mine = lane_head == first_head + k
        query = jnp.where(mine, queries, 0.0).astype(BF16)
        scores = dot_nt(query, key_rows) * (HEAD_DIM**-0.5) + key_shift[k : k + 1, :]
        weights = jnp.exp(scores - jnp.max(scores, axis=1, keepdims=True))
        soft = (weights * (1.0 / jnp.sum(weights, axis=1, keepdims=True))).astype(BF16)
        part = dot(soft, jnp.where(mine, values, 0.0).astype(BF16))
        total = part if total is None else total + part
    total = total.reshape(R, PR, LANES)
    sendo[:, 0:PR, :] = total.astype(BF16)
    above = jnp.concatenate([total[R - 1 : R], total[0 : R - 1]], axis=0)[:, PR - 1 : PR, :]
    below = jnp.concatenate([total[1:R], total[0:1]], axis=0)[:, 0:1, :]
    sendo[:, PR : 2 * PR, :] = jnp.where(
        place == 0, above, jnp.where(place == 1, below, 0.0)
    ).astype(BF16)
    o_source = lambda peer: sendo.at[peer]
    exchange("start", o_source, recvo, o_ss, o_rs)
    recvo[row] = sendo[row]
    edge_copies("recv")
    halo_copies("send")
    col_copies(0, "send")
    exchange("send", k_source, recvk, k_ss, k_rs)
    exchange("send", q_source, recvq, q_ss, q_rs)
    edge_copies("send")
    exchange("recv", o_source, recvo, o_ss, o_rs)

    back = recvo[...].reshape(NP, GH, split, 2 * PR, LANES)
    sides = []
    for g in range(GH):
        share = back[:, g, 0]
        for s in range(1, split):
            share = share + back[:, g, s]
        sides.append(share.reshape(NP * 2 * PR, LANES))
    attended = jnp.concatenate(sides, axis=1)
    change = dot(attended, outw_v[...]).reshape(NP, 2 * PR, D)
    updated = (tokens + change[:, 0:PR, :]).reshape(NP * PR, D).astype(BF16)
    for way, i in ((0, PATCH - 1), (1, 0)):
        outer = (halo2[way, 0:NP, :] + change[:, PR + way, :]).astype(BF16)
        outer = halo2[way, NP : 2 * NP, :] + dot_nt(outer, unp_i[i])
        outer = jnp.where(row_ok[2 * way - 1], outer, 0.0).astype(BF16).astype(F32)
        for p in range(NP):
            tmap[1, p + 1, way * (TOP + L) : way * (TOP + L) + TOP, :] = jnp.broadcast_to(
                outer[p : p + 1, :], (TOP, CJ)
            )
    for i in range(PATCH):
        expanded = dot_nt(updated, unp_i[i])
        for half in range(2):
            wide[half, pl.ds(i, NP * PR, stride=PATCH), :] = expanded[
                :, half * LANES : (half + 1) * LANES
            ]

    def merge(p):
        for half in range(2):
            cells = mixed[half, p * L : (p + 1) * L, :] + wide[half, p * L : (p + 1) * L, :]
            tmap[1, p + 1, TOP : TOP + L, half * LANES : (half + 1) * LANES] = cells.astype(
                BF16
            ).astype(F32)

    merge(0)
    merge(NP - 1)
    col_copies(1, "start")
    for p in range(1, NP - 1):
        merge(p)
    exchange("send", o_source, recvo, o_ss, o_rs)

    def finish(blocks):
        second = conv(1, blocks)
        return [
            (tmap[1, p + 1, TOP : TOP + L, :] + second[n]).T.reshape(C, PATCH, L)
            for n, p in enumerate(blocks)
        ]

    def put(q, top, bottom):
        o_ref[:, 2 * PATCH * q : 2 * PATCH * (q + 1), :] = jnp.concatenate(
            [top, bottom], axis=1
        ).astype(BF16)

    inside = finish(middle_blocks)
    for q in range(1, NP // 2 - 1):
        put(q, inside[2 * q - 1], inside[2 * q])
    col_copies(1, "recv")
    outside = finish(outer_blocks)
    put(0, outside[0], inside[0])
    put(NP // 2 - 1, inside[NP - 3], outside[1])
    col_copies(1, "send")


def per_device(
    R, NC, pair_map, conv_in, embed_weight, qkv_weight, key_bias, out_weight, unpatch, conv_out
):
    NP = pair_map.shape[1] // PATCH
    L = pair_map.shape[2]
    PR = L // PATCH
    CJ = C * PATCH
    groups = NP * (D // LANES)
    hbm = pl.BlockSpec(memory_space=pltpu.HBM)
    dma = pltpu.SemaphoreType.DMA
    inputs = (
        pair_map,
        key_bias.transpose(1, 2, 0),
        conv_in,
        conv_out,
        embed_weight,
        qkv_weight,
        out_weight,
        unpatch,
    )
    return pl.pallas_call(
        functools.partial(trunk_kernel, R, NC),
        out_shape=pltpu.VMEM(pair_map.shape, BF16),
        in_specs=[hbm] * 8,
        out_specs=pl.BlockSpec(memory_space=pltpu.VMEM),
        scratch_shapes=[pltpu.VMEM(a.shape, BF16) for a in inputs]
        + [
            pltpu.VMEM((2, NP + 2, L + 2 * TOP, CJ), F32),
            pltpu.VMEM((2, NP * L, LANES), F32),
            pltpu.VMEM((2, NP, CJ), F32),
            pltpu.VMEM((2, 3, NP, CJ), F32),
            pltpu.VMEM((2, 2 * NP, CJ), F32),
            pltpu.VMEM((2, 2 * NP, CJ), F32),
            pltpu.VMEM((2, CJ * PATCH, LANES), F32),
            pltpu.VMEM((PATCH, CJ, D), BF16),
            pltpu.VMEM((PATCH, CJ, D), BF16),
            pltpu.VMEM((2, 3, 2 * CJ, CJ), BF16),
            pltpu.VMEM((PR, LANES), BF16),
            pltpu.VMEM((R, PR, LANES), BF16),
            pltpu.VMEM((groups, PR, 3 * LANES), BF16),
            pltpu.VMEM((R, PR, 3 * LANES), BF16),
            pltpu.VMEM((R, 2 * PR, LANES), BF16),
            pltpu.VMEM((R, 2 * PR, LANES), BF16),
            dma((NP // 2,)),
            dma((7,)),
            dma((2, 3)),
            dma((2, 3)),
            dma((2, 2)),
            dma((2, 2)),
            dma((2,)),
            dma((2,)),
            dma((R,)),
            dma((R,)),
            dma((R,)),
            dma((R,)),
            dma((R,)),
            dma((R,)),
            pltpu.SemaphoreType.REGULAR,
        ],
        compiler_params=pltpu.CompilerParams(
            collective_id=0, has_side_effects=True, vmem_limit_bytes=VMEM_BYTES
        ),
    )(*inputs)


def solution(mesh):
    placed = (P(None, "cols", "rows"), P(), P(), P(), P("rows", "cols", None), P(), P(), P())
    return jax.shard_map(
        functools.partial(per_device, mesh.shape["rows"], mesh.shape["cols"]),
        mesh=mesh,
        in_specs=placed,
        out_specs=P(None, "cols", "rows"),
        check_vma=False,
    )
```

```python
import functools

import jax
import jax.numpy as jnp
from jax import lax
from jax.experimental import pallas as pl
from jax.experimental.pallas import tpu as pltpu
from jax.sharding import PartitionSpec as P

C = 32
PATCH = 8
D = 256
HEADS = 8
HEAD_DIM = 32
LANES = 128
EPSILON = 1e-05
F32 = jnp.float32
BF16 = jnp.bfloat16
MESH = pl.DeviceIdType.MESH
NT = (((1,), (1,)), ((), ()))
TOP = 8
VMEM_BYTES = 56 * 1024 * 1024


def dot(a, b):
    return jnp.dot(a, b, preferred_element_type=F32)


def dot_nt(a, b):
    return lax.dot_general(a, b, NT, preferred_element_type=F32)


def iota(shape, dim):
    return lax.broadcasted_iota(jnp.int32, shape, dim)


def trunk_kernel(
    R,
    NC,
    x_hbm,
    kb_hbm,
    cin_hbm,
    cout_hbm,
    embed_hbm,
    qkv_hbm,
    outw_hbm,
    unp_hbm,
    o_ref,
    x_v,
    kb_v,
    cin_v,
    cout_v,
    embed_v,
    qkv_v,
    outw_v,
    unp_v,
    tmap,
    mixed,
    edges,
    halo,
    edges2,
    halo2,
    wide,
    embed_i,
    unp_i,
    taps,
    sendk,
    recvk,
    sendq,
    recvq,
    sendo,
    recvo,
    x_sem,
    load_sem,
    halo_ss,
    halo_rs,
    col_ss,
    col_rs,
    h2_ss,
    h2_rs,
    k_ss,
    k_rs,
    q_ss,
    q_rs,
    o_ss,
    o_rs,
    met,
):
    row = lax.axis_index("rows")
    col = lax.axis_index("cols")
    NP = x_v.shape[1] // PATCH
    L = x_v.shape[2]
    PR = L // PATCH
    CJ = C * PATCH
    GH = D // LANES
    groups = NP * GH
    split = R // groups
    group_heads = LANES // HEAD_DIM
    my_heads = group_heads // split
    keys = R * PR
    bits = R.bit_length() - 1
    low = 2 ** (bits // 2)

    row_ok = {-1: row > 0, 1: row < R - 1}
    col_ok = {-1: col > 0, 0: col >= 0, 1: col < NC - 1}
    barrier = pltpu.get_barrier_semaphore()

    def partner(k):
        return row + (1 - 2 * lax.rem(row // 2**k, 2)) * 2**k

    flips = [partner(k) - row for k in range(bits)]

    def peer_at(d):
        peer = row
        for k in range(bits):
            if d // 2**k % 2:
                peer = peer + flips[k]
        return peer

    def greet(peer_row, peer_col):
        pl.semaphore_signal(
            barrier,
            inc=1,
            device_id={"rows": peer_row, "cols": peer_col},
            device_id_type=MESH,
        )

    lines = list(range(R - low, 0, -low)) + list(range(low - 1, 0, -1))
    for d in lines:
        greet(peer_at(d), col)
    expected = len(lines)
    for dr in (-1, 1):
        expected = expected + row_ok[dr].astype(jnp.int32)

        @pl.when(row_ok[dr])
        def _():
            greet(row + dr, col)

    for dc in (-1, 1):
        for dr in (-1, 0, 1):
            ok = col_ok[dc] if dr == 0 else jnp.logical_and(col_ok[dc], row_ok[dr])
            expected = expected + ok.astype(jnp.int32)

            @pl.when(ok)
            def _():
                greet(row + dr, col + dc)

    x_loads = [
        pltpu.make_async_copy(
            x_hbm.at[:, pl.ds(2 * PATCH * q, 2 * PATCH), :],
            x_v.at[:, pl.ds(2 * PATCH * q, 2 * PATCH), :],
            x_sem.at[q],
        )
        for q in range(NP // 2)
    ]
    loads = [
        pltpu.make_async_copy(src, dst, load_sem.at[n])
        for n, (src, dst) in enumerate(
            (
                (cin_hbm, cin_v),
                (embed_hbm, embed_v),
                (kb_hbm, kb_v),
                (qkv_hbm, qkv_v),
                (unp_hbm, unp_v),
                (cout_hbm, cout_v),
                (outw_hbm, outw_v),
            )
        )
    ]
    cin_load, embed_load, kb_load, qkv_load, unp_load, cout_load, outw_load = loads
    for copy in (cin_load, kb_load, *x_loads, embed_load, qkv_load, unp_load, cout_load, outw_load):
        copy.start()

    def banded(n, weight):
        spread = (iota((CJ, C), 0) // PATCH == iota((CJ, C), 1)).astype(F32).astype(BF16)
        wide_weight = dot(spread, weight).astype(BF16)
        shift = iota((CJ, CJ), 0) % PATCH - iota((CJ, CJ), 1) % PATCH
        ahead = iota((CJ, 9 * C), 1) - iota((CJ, 9 * C), 0) // PATCH
        for b in range(3):
            centre = jnp.zeros((CJ, CJ), F32)
            rim = jnp.zeros((CJ, CJ), F32)
            for a in range(3):
                start = (3 * a + b) * C
                lanes = slice(0, CJ) if start < CJ else slice(CJ, 9 * C)
                pick = (ahead[:, lanes] == start).astype(F32).astype(BF16)
                full = dot_nt(pick, wide_weight[:, lanes])
                centre = jnp.where(shift == a - 1, full, centre)
                if a == 0:
                    rim = jnp.where(shift == PATCH - 1, full, rim)
                if a == 2:
                    rim = jnp.where(shift == 1 - PATCH, full, rim)
            taps[n, b, 0:CJ, :] = centre.astype(BF16)
            taps[n, b, CJ : 2 * CJ, :] = rim.astype(BF16)

    cin_load.wait()
    banded(0, cin_v[...])

    kb_load.wait()
    same = (iota((PR, PR), 0) == iota((PR, PR), 1)).astype(F32).astype(BF16)
    bias = dot_nt(same, kb_v[...].astype(F32).reshape(NP * HEADS, PR).astype(BF16))
    pad = jnp.zeros((PR, LANES - NP * HEADS), F32)
    sendk[...] = jnp.concatenate([bias, pad], axis=1).astype(BF16)

    for q in range(NP // 2):
        x_loads[q].wait()
        pair = x_v[:, 2 * PATCH * q : 2 * PATCH * (q + 1), :].astype(F32)
        for s in range(2):
            block = pair[:, PATCH * s : PATCH * (s + 1), :].reshape(CJ, L)
            tmap[0, 1 + 2 * q + s, TOP : TOP + L, :] = block.T
    for p in range(NP):
        edges[0, p : p + 1, :] = tmap[0, p + 1, TOP + L - 1 : TOP + L, :]
        edges[1, p : p + 1, :] = tmap[0, p + 1, TOP : TOP + 1, :]

    for way, dr in ((0, -1), (1, 1)):
        for slot in range(3):
            missing = jnp.logical_not(jnp.logical_and(row_ok[dr], col_ok[slot - 1]))

            @pl.when(missing)
            def _():
                halo[way, slot] = jnp.zeros((NP, CJ), F32)

        @pl.when(jnp.logical_not(row_ok[dr]))
        def _():
            halo2[way] = jnp.zeros((2 * NP, CJ), F32)

    for side, dc in ((0, -1), (1, 1)):

        @pl.when(jnp.logical_not(col_ok[dc]))
        def _():
            tmap[0, side * (NP + 1), TOP : TOP + L, :] = jnp.zeros((L, CJ), F32)
            tmap[1, side * (NP + 1), :, :] = jnp.zeros((L + 2 * TOP, CJ), F32)

    tmap[0, :, 0:TOP, :] = jnp.zeros((NP + 2, TOP, CJ), F32)
    tmap[0, :, TOP + L : L + 2 * TOP, :] = jnp.zeros((NP + 2, TOP, CJ), F32)

    pl.semaphore_wait(barrier, expected)

    for d in range(1, low):
        pl.semaphore_signal(
            met, inc=1, device_id={"rows": peer_at(d), "cols": col}, device_id_type=MESH
        )

    def act_on(copy, act):
        if act == "start":
            copy.start()
        elif act == "send":
            copy.wait_send()
        else:
            copy.wait_recv()

    def col_copies(phase, act):
        place = pl.ds(TOP, L) if phase == 0 else pl.ds(0, L + 2 * TOP)
        for side, dc in ((0, 1), (1, -1)):
            copy = pltpu.make_async_remote_copy(
                src_ref=tmap.at[phase, NP if side == 0 else 1, place],
                dst_ref=tmap.at[phase, 0 if side == 0 else NP + 1, place],
                send_sem=col_ss.at[phase, side],
                recv_sem=col_rs.at[phase, side],
                device_id={"rows": row, "cols": col + (-dc if act == "recv" else dc)},
                device_id_type=MESH,
            )
            ok = col_ok[-dc] if act == "recv" else col_ok[dc]

            @pl.when(ok)
            def _():
                act_on(copy, act)

    def halo_copies(act):
        for way, dr in ((0, 1), (1, -1)):
            for slot in range(3):
                dc = slot - 1
                if act == "recv":
                    ok = jnp.logical_and(row_ok[-dr], col_ok[dc])
                    peer = {"rows": row - dr, "cols": col + dc}
                else:
                    ok = jnp.logical_and(row_ok[dr], col_ok[-dc])
                    peer = {"rows": row + dr, "cols": col - dc}
                copy = pltpu.make_async_remote_copy(
                    src_ref=edges.at[way],
                    dst_ref=halo.at[way, slot],
                    send_sem=halo_ss.at[way, slot],
                    recv_sem=halo_rs.at[way, slot],
                    device_id=peer,
                    device_id_type=MESH,
                )

                @pl.when(ok)
                def _():
                    act_on(copy, act)

    def edge_copies(act):
        for way, dr in ((0, 1), (1, -1)):
            copy = pltpu.make_async_remote_copy(
                src_ref=edges2.at[way],
                dst_ref=halo2.at[way],
                send_sem=h2_ss.at[way],
                recv_sem=h2_rs.at[way],
                device_id={"rows": row + (-dr if act == "recv" else dr), "cols": col},
                device_id_type=MESH,
            )

            @pl.when(row_ok[-dr] if act == "recv" else row_ok[dr])
            def _():
                act_on(copy, act)

    def exchange(act, source, target, send_sem, recv_sem):
        for d in range(R - 1, 0, -1):
            peer = peer_at(d)
            copy = pltpu.make_async_remote_copy(
                src_ref=source(peer),
                dst_ref=target.at[peer if act == "recv" else row],
                send_sem=send_sem.at[peer],
                recv_sem=recv_sem.at[peer if act == "recv" else row],
                device_id={"rows": peer, "cols": col},
                device_id_type=MESH,
            )
            act_on(copy, act)

    halo_copies("start")
    col_copies(0, "start")
    lane_place = iota((1, CJ), 1) % PATCH

    def rim_of(before, after):
        after = jnp.where(lane_place == 0, after, jnp.zeros_like(after))
        return jnp.where(lane_place == PATCH - 1, before, after)

    def conv(phase, blocks):
        count = len(blocks)
        near = sorted({p + d for p in blocks for d in range(3)})
        parts = []
        for b in range(3):
            rows = slice(TOP - 1 + b, TOP - 1 + b + L)
            cells = {p: tmap[phase, p, rows, :].astype(BF16) for p in near}
            parts.append(jnp.concatenate([cells[p + 1] for p in blocks], axis=0))
            rims = [rim_of(cells[p], cells[p + 2]) for p in blocks]
            parts.append(jnp.concatenate(rims, axis=0))
        total = dot(jnp.concatenate(parts, axis=1), taps[phase].reshape(6 * CJ, CJ))
        return total.reshape(count, L, CJ)

    def silu(v):
        return v * (0.5 + 0.5 * jnp.tanh(0.5 * v))

    embed_load.wait()
    for half in range(2):
        wide[half] = embed_v[:, half * LANES : (half + 1) * LANES].astype(F32)
    for i in range(PATCH):
        for half in range(2):
            embed_i[i, :, half * LANES : (half + 1) * LANES] = wide[
                half, pl.ds(i, CJ, stride=PATCH), :
            ].astype(BF16)

    edge_conv = ([None] * NP, [None] * NP)

    middle_blocks = list(range(1, NP - 1))
    outer_blocks = [0, NP - 1]

    def mix(blocks):
        inner = conv(0, blocks)
        for n, p in enumerate(blocks):
            base = tmap[0, p + 1, TOP : TOP + L, :]
            cells = (base + silu(inner[n])).astype(BF16).astype(F32)
            for half in range(2):
                mixed[half, p * L : (p + 1) * L, :] = cells[:, half * LANES : (half + 1) * LANES]
            edge_conv[0][p] = inner[n, 0:1, :]
            edge_conv[1][p] = inner[n, L - 1 : L, :]

    mix(middle_blocks)
    col_copies(0, "recv")
    if low > 1:
        pl.semaphore_wait(met, low - 1)
    k_source = lambda peer: sendk
    exchange("start", k_source, recvk, k_ss, k_rs)
    mix(outer_blocks)
    edge_conv = [jnp.concatenate(rows, axis=0) for rows in edge_conv]

    def embed(i, rows):
        return dot(rows.astype(BF16), embed_i[i])

    def normalise(tokens):
        mean = jnp.mean(tokens, axis=1, keepdims=True)
        centred = tokens - mean
        var = jnp.mean(centred * centred, axis=1, keepdims=True)
        return (centred * lax.rsqrt(var + EPSILON)).astype(BF16)

    cells = []
    for i in range(PATCH):
        halves = [mixed[half, pl.ds(i, NP * PR, stride=PATCH), :] for half in range(2)]
        cells.append(jnp.concatenate(halves, axis=1).astype(BF16))
    middle = dot(
        jnp.concatenate(cells[1 : PATCH - 1], axis=1),
        embed_i[1 : PATCH - 1].reshape((PATCH - 2) * CJ, D),
    )
    parts = {i: embed(i, cells[i]) for i in (0, PATCH - 1)}
    inner = (middle + parts[0] + parts[PATCH - 1]).astype(BF16).astype(F32)
    partial = (
        (middle + parts[PATCH - 1]).reshape(NP, PR, D)[:, 0, :],
        (middle + parts[0]).reshape(NP, PR, D)[:, PR - 1, :],
    )

    halo_copies("recv")
    edge_tokens = []
    for way, cell, tap in ((0, 0, 0), (1, L - 1, 2)):
        centre = halo[way, 1]
        before = jnp.concatenate([halo[way, 0, NP - 1 : NP, :], centre[0 : NP - 1]], axis=0)
        after = jnp.concatenate([centre[1:NP], halo[way, 2, 0:1, :]], axis=0)
        rim = rim_of(before, after)
        extra = dot(centre.astype(BF16), taps[0, tap, 0:CJ, :])
        extra = extra + dot(rim.astype(BF16), taps[0, tap, CJ : 2 * CJ, :])
        fixed = (edges[1 - way] + silu(edge_conv[way] + extra)).astype(BF16).astype(F32)
        for half in range(2):
            mixed[half, pl.ds(cell, NP, stride=L), :] = fixed[:, half * LANES : (half + 1) * LANES]
        edge_token = partial[way] + embed(way * (PATCH - 1), fixed)
        edge_token = edge_token.astype(BF16).astype(F32)
        edge_tokens.append(edge_token)
        edges2[1 - way, 0:NP, :] = edge_token
        edges2[1 - way, NP : 2 * NP, :] = fixed
    place = iota((1, PR, 1), 1)
    tokens = jnp.where(
        place == 0,
        edge_tokens[0][:, None, :],
        jnp.where(place == PR - 1, edge_tokens[1][:, None, :], inner.reshape(NP, PR, D)),
    )

    qkv_load.wait()
    projected = dot(normalise(tokens.reshape(NP * PR, D)), qkv_v[...]).astype(BF16)
    for g in range(GH):
        for kind in range(3):
            start = kind * D + g * LANES
            part = projected[:, start : start + LANES].reshape(NP, PR, LANES)
            for p in range(NP):
                sendq[p * GH + g, :, kind * LANES : (kind + 1) * LANES] = part[p]
    q_source = lambda peer: sendq.at[peer // split]
    exchange("start", q_source, recvq, q_ss, q_rs)
    edge_copies("start")
    recvq[row] = sendq[row // split]
    recvk[row] = sendk[...]

    unp_load.wait()
    for k in range(PATCH):
        block = unp_v[:, k * CJ : (k + 1) * CJ].astype(F32).T
        for half in range(2):
            wide[half, k * CJ : (k + 1) * CJ, :] = block[:, half * LANES : (half + 1) * LANES]
    for i in range(PATCH):
        for half in range(2):
            unp_i[i, :, half * LANES : (half + 1) * LANES] = wide[
                half, pl.ds(i, CJ, stride=PATCH), :
            ].astype(BF16)

    cout_load.wait()
    banded(1, cout_v[...])
    outw_load.wait()
    exchange("recv", k_source, recvk, k_ss, k_rs)
    first_head = lax.rem(row, split) * my_heads
    first_global = (row // split) * group_heads + first_head
    pick = (iota((16, LANES), 1) == iota((16, LANES), 0) + first_global).astype(F32).astype(BF16)
    key_shift = dot_nt(pick, recvk[...].reshape(keys, LANES))
    exchange("recv", q_source, recvq, q_ss, q_rs)

    queries = recvq[:, :, 0:LANES].astype(F32).reshape(keys, LANES)
    key_rows = recvq[:, :, LANES : 2 * LANES].reshape(keys, LANES)
    values = recvq[:, :, 2 * LANES : 3 * LANES].astype(F32).reshape(keys, LANES)
    lane_head = iota((1, LANES), 1) // HEAD_DIM
    softs, parts = [], []
    for k in range(my_heads):
        mine = lane_head == first_head + k
        query = jnp.where(mine, queries, 0.0).astype(BF16)
        scores = dot_nt(query, key_rows) * (HEAD_DIM**-0.5) + key_shift[k : k + 1, :]
        weights = jnp.exp(scores - jnp.max(scores, axis=1, keepdims=True))
        softs.append((weights * (1.0 / jnp.sum(weights, axis=1, keepdims=True))).astype(BF16))
        parts.append(jnp.where(mine, values, 0.0).astype(BF16))
    total = dot(jnp.concatenate(softs, axis=1), jnp.concatenate(parts, axis=0))
    total = total.reshape(R, PR, LANES)
    sendo[:, 0:PR, :] = total.astype(BF16)
    above = jnp.concatenate([total[R - 1 : R], total[0 : R - 1]], axis=0)[:, PR - 1 : PR, :]
    below = jnp.concatenate([total[1:R], total[0:1]], axis=0)[:, 0:1, :]
    sendo[:, PR : 2 * PR, :] = jnp.where(
        place == 0, above, jnp.where(place == 1, below, 0.0)
    ).astype(BF16)
    o_source = lambda peer: sendo.at[peer]
    exchange("start", o_source, recvo, o_ss, o_rs)
    recvo[row] = sendo[row]
    edge_copies("recv")
    halo_copies("send")
    col_copies(0, "send")
    exchange("send", k_source, recvk, k_ss, k_rs)
    exchange("send", q_source, recvq, q_ss, q_rs)
    edge_copies("send")
    exchange("recv", o_source, recvo, o_ss, o_rs)

    back = recvo[...].reshape(NP, GH, split, 2 * PR, LANES)
    sides = []
    for g in range(GH):
        share = back[:, g, 0]
        for s in range(1, split):
            share = share + back[:, g, s]
        sides.append(share.reshape(NP * 2 * PR, LANES))
    attended = jnp.concatenate(sides, axis=1)
    change = dot(attended, outw_v[...]).reshape(NP, 2 * PR, D)
    updated = (tokens + change[:, 0:PR, :]).reshape(NP * PR, D).astype(BF16)
    for way, i in ((0, PATCH - 1), (1, 0)):
        outer = (halo2[way, 0:NP, :] + change[:, PR + way, :]).astype(BF16)
        outer = halo2[way, NP : 2 * NP, :] + dot_nt(outer, unp_i[i])
        outer = jnp.where(row_ok[2 * way - 1], outer, 0.0).astype(BF16).astype(F32)
        for p in range(NP):
            tmap[1, p + 1, way * (TOP + L) : way * (TOP + L) + TOP, :] = jnp.broadcast_to(
                outer[p : p + 1, :], (TOP, CJ)
            )
    for i in range(PATCH):
        expanded = dot_nt(updated, unp_i[i])
        for half in range(2):
            wide[half, pl.ds(i, NP * PR, stride=PATCH), :] = expanded[
                :, half * LANES : (half + 1) * LANES
            ]

    def merge(p):
        for half in range(2):
            cells = mixed[half, p * L : (p + 1) * L, :] + wide[half, p * L : (p + 1) * L, :]
            tmap[1, p + 1, TOP : TOP + L, half * LANES : (half + 1) * LANES] = cells.astype(
                BF16
            ).astype(F32)

    merge(0)
    merge(NP - 1)
    col_copies(1, "start")
    for p in range(1, NP - 1):
        merge(p)
    exchange("send", o_source, recvo, o_ss, o_rs)

    def finish(blocks, second):
        return {
            p: (tmap[1, p + 1, TOP : TOP + L, :] + second[n]).T.reshape(C, PATCH, L)
            for n, p in enumerate(blocks)
        }

    def put(q, top, bottom):
        o_ref[:, 2 * PATCH * q : 2 * PATCH * (q + 1), :] = jnp.concatenate(
            [top, bottom], axis=1
        ).astype(BF16)

    inside = conv(1, middle_blocks)
    col_copies(1, "recv")
    outside = conv(1, outer_blocks)
    done = finish(middle_blocks, inside) | finish(outer_blocks, outside)
    for q in range(NP // 2):
        put(q, done[2 * q], done[2 * q + 1])
    col_copies(1, "send")


def per_device(
    R, NC, pair_map, conv_in, embed_weight, qkv_weight, key_bias, out_weight, unpatch, conv_out
):
    NP = pair_map.shape[1] // PATCH
    L = pair_map.shape[2]
    PR = L // PATCH
    CJ = C * PATCH
    groups = NP * (D // LANES)
    hbm = pl.BlockSpec(memory_space=pltpu.HBM)
    dma = pltpu.SemaphoreType.DMA
    inputs = (
        pair_map,
        key_bias.transpose(1, 2, 0),
        conv_in,
        conv_out,
        embed_weight,
        qkv_weight,
        out_weight,
        unpatch,
    )
    return pl.pallas_call(
        functools.partial(trunk_kernel, R, NC),
        out_shape=pltpu.VMEM(pair_map.shape, BF16),
        in_specs=[hbm] * 8,
        out_specs=pl.BlockSpec(memory_space=pltpu.VMEM),
        scratch_shapes=[pltpu.VMEM(a.shape, BF16) for a in inputs]
        + [
            pltpu.VMEM((2, NP + 2, L + 2 * TOP, CJ), F32),
            pltpu.VMEM((2, NP * L, LANES), F32),
            pltpu.VMEM((2, NP, CJ), F32),
            pltpu.VMEM((2, 3, NP, CJ), F32),
            pltpu.VMEM((2, 2 * NP, CJ), F32),
            pltpu.VMEM((2, 2 * NP, CJ), F32),
            pltpu.VMEM((2, CJ * PATCH, LANES), F32),
            pltpu.VMEM((PATCH, CJ, D), BF16),
            pltpu.VMEM((PATCH, CJ, D), BF16),
            pltpu.VMEM((2, 3, 2 * CJ, CJ), BF16),
            pltpu.VMEM((PR, LANES), BF16),
            pltpu.VMEM((R, PR, LANES), BF16),
            pltpu.VMEM((groups, PR, 3 * LANES), BF16),
            pltpu.VMEM((R, PR, 3 * LANES), BF16),
            pltpu.VMEM((R, 2 * PR, LANES), BF16),
            pltpu.VMEM((R, 2 * PR, LANES), BF16),
            dma((NP // 2,)),
            dma((7,)),
            dma((2, 3)),
            dma((2, 3)),
            dma((2, 2)),
            dma((2, 2)),
            dma((2,)),
            dma((2,)),
            dma((R,)),
            dma((R,)),
            dma((R,)),
            dma((R,)),
            dma((R,)),
            dma((R,)),
            pltpu.SemaphoreType.REGULAR,
        ],
        compiler_params=pltpu.CompilerParams(
            collective_id=0, has_side_effects=True, vmem_limit_bytes=VMEM_BYTES
        ),
    )(*inputs)


def solution(mesh):
    placed = (P(None, "cols", "rows"), P(), P(), P(), P("rows", "cols", None), P(), P(), P())
    return jax.shard_map(
        functools.partial(per_device, mesh.shape["rows"], mesh.shape["cols"]),
        mesh=mesh,
        in_specs=placed,
        out_specs=P(None, "cols", "rows"),
        check_vma=False,
    )
```

```python
import functools

import jax
import jax.numpy as jnp
from jax import lax
from jax.experimental import pallas as pl
from jax.experimental.pallas import tpu as pltpu
from jax.sharding import PartitionSpec as P

C = 32
PATCH = 8
D = 256
HEADS = 8
HEAD_DIM = 32
LANES = 128
EPSILON = 1e-05
F32 = jnp.float32
BF16 = jnp.bfloat16
MESH = pl.DeviceIdType.MESH
NT = (((1,), (1,)), ((), ()))
TOP = 8
VMEM_BYTES = 56 * 1024 * 1024


def dot(a, b):
    return jnp.dot(a, b, preferred_element_type=F32)


def dot_nt(a, b):
    return lax.dot_general(a, b, NT, preferred_element_type=F32)


def iota(shape, dim):
    return lax.broadcasted_iota(jnp.int32, shape, dim)


def trunk_kernel(
    R,
    NC,
    x_hbm,
    kb_hbm,
    cin_hbm,
    cout_hbm,
    embed_hbm,
    qkv_hbm,
    outw_hbm,
    unp_hbm,
    o_ref,
    x_v,
    kb_v,
    cin_v,
    cout_v,
    embed_v,
    qkv_v,
    outw_v,
    unp_v,
    tmap,
    mixed,
    edges,
    halo,
    edges2,
    halo2,
    wide,
    embed_i,
    unp_i,
    taps,
    sendk,
    recvk,
    sendq,
    recvq,
    sendo,
    recvo,
    x_sem,
    load_sem,
    halo_ss,
    halo_rs,
    col_ss,
    col_rs,
    h2_ss,
    h2_rs,
    k_ss,
    k_rs,
    q_ss,
    q_rs,
    o_ss,
    o_rs,
    met,
):
    row = lax.axis_index("rows")
    col = lax.axis_index("cols")
    NP = x_v.shape[1] // PATCH
    L = x_v.shape[2]
    PR = L // PATCH
    CJ = C * PATCH
    GH = D // LANES
    groups = NP * GH
    split = R // groups
    group_heads = LANES // HEAD_DIM
    my_heads = group_heads // split
    keys = R * PR
    bits = R.bit_length() - 1
    low = 2 ** (bits // 2)

    row_ok = {-1: row > 0, 1: row < R - 1}
    col_ok = {-1: col > 0, 0: col >= 0, 1: col < NC - 1}
    barrier = pltpu.get_barrier_semaphore()

    def partner(k):
        return row + (1 - 2 * lax.rem(row // 2**k, 2)) * 2**k

    flips = [partner(k) - row for k in range(bits)]

    def peer_at(d):
        peer = row
        for k in range(bits):
            if d // 2**k % 2:
                peer = peer + flips[k]
        return peer

    def greet(peer_row, peer_col):
        pl.semaphore_signal(
            barrier,
            inc=1,
            device_id={"rows": peer_row, "cols": peer_col},
            device_id_type=MESH,
        )

    lines = list(range(R - low, 0, -low)) + list(range(low - 1, 0, -1))
    for d in lines:
        greet(peer_at(d), col)
    expected = len(lines)
    for dr in (-1, 1):
        expected = expected + row_ok[dr].astype(jnp.int32)

        @pl.when(row_ok[dr])
        def _():
            greet(row + dr, col)

    for dc in (-1, 1):
        for dr in (-1, 0, 1):
            ok = col_ok[dc] if dr == 0 else jnp.logical_and(col_ok[dc], row_ok[dr])
            expected = expected + ok.astype(jnp.int32)

            @pl.when(ok)
            def _():
                greet(row + dr, col + dc)

    x_loads = [
        pltpu.make_async_copy(
            x_hbm.at[:, pl.ds(2 * PATCH * q, 2 * PATCH), :],
            x_v.at[:, pl.ds(2 * PATCH * q, 2 * PATCH), :],
            x_sem.at[q],
        )
        for q in range(NP // 2)
    ]
    loads = [
        pltpu.make_async_copy(src, dst, load_sem.at[n])
        for n, (src, dst) in enumerate(
            (
                (cin_hbm, cin_v),
                (embed_hbm, embed_v),
                (kb_hbm, kb_v),
                (qkv_hbm, qkv_v),
                (unp_hbm, unp_v),
                (cout_hbm, cout_v),
                (outw_hbm, outw_v),
            )
        )
    ]
    cin_load, embed_load, kb_load, qkv_load, unp_load, cout_load, outw_load = loads
    for copy in (cin_load, kb_load, *x_loads, embed_load, qkv_load, unp_load, cout_load, outw_load):
        copy.start()

    def banded(n, weight):
        spread = (iota((CJ, C), 0) // PATCH == iota((CJ, C), 1)).astype(F32).astype(BF16)
        wide_weight = dot(spread, weight).astype(BF16)
        shift = iota((CJ, CJ), 0) % PATCH - iota((CJ, CJ), 1) % PATCH
        ahead = iota((CJ, 9 * C), 1) - iota((CJ, 9 * C), 0) // PATCH
        for b in range(3):
            centre = jnp.zeros((CJ, CJ), F32)
            rim = jnp.zeros((CJ, CJ), F32)
            for a in range(3):
                start = (3 * a + b) * C
                lanes = slice(0, CJ) if start < CJ else slice(CJ, 9 * C)
                pick = (ahead[:, lanes] == start).astype(F32).astype(BF16)
                full = dot_nt(pick, wide_weight[:, lanes])
                centre = jnp.where(shift == a - 1, full, centre)
                if a == 0:
                    rim = jnp.where(shift == PATCH - 1, full, rim)
                if a == 2:
                    rim = jnp.where(shift == 1 - PATCH, full, rim)
            taps[n, b, 0:CJ, :] = centre.astype(BF16)
            taps[n, b, CJ : 2 * CJ, :] = rim.astype(BF16)

    cin_load.wait()
    banded(0, cin_v[...])

    kb_load.wait()
    same = (iota((PR, PR), 0) == iota((PR, PR), 1)).astype(F32).astype(BF16)
    bias = dot_nt(same, kb_v[...].astype(F32).reshape(NP * HEADS, PR).astype(BF16))
    pad = jnp.zeros((PR, LANES - NP * HEADS), F32)
    sendk[...] = jnp.concatenate([bias, pad], axis=1).astype(BF16)

    for q in range(NP // 2):
        x_loads[q].wait()
        pair = x_v[:, 2 * PATCH * q : 2 * PATCH * (q + 1), :].astype(F32)
        for s in range(2):
            block = pair[:, PATCH * s : PATCH * (s + 1), :].reshape(CJ, L)
            tmap[0, 1 + 2 * q + s, TOP : TOP + L, :] = block.T
    for p in range(NP):
        edges[0, p : p + 1, :] = tmap[0, p + 1, TOP + L - 1 : TOP + L, :]
        edges[1, p : p + 1, :] = tmap[0, p + 1, TOP : TOP + 1, :]

    for way, dr in ((0, -1), (1, 1)):
        for slot in range(3):
            missing = jnp.logical_not(jnp.logical_and(row_ok[dr], col_ok[slot - 1]))

            @pl.when(missing)
            def _():
                halo[way, slot] = jnp.zeros((NP, CJ), F32)

        @pl.when(jnp.logical_not(row_ok[dr]))
        def _():
            halo2[way] = jnp.zeros((2 * NP, CJ), F32)

    for side, dc in ((0, -1), (1, 1)):

        @pl.when(jnp.logical_not(col_ok[dc]))
        def _():
            tmap[0, side * (NP + 1), TOP : TOP + L, :] = jnp.zeros((L, CJ), F32)
            tmap[1, side * (NP + 1), :, :] = jnp.zeros((L + 2 * TOP, CJ), F32)

    tmap[0, :, 0:TOP, :] = jnp.zeros((NP + 2, TOP, CJ), F32)
    tmap[0, :, TOP + L : L + 2 * TOP, :] = jnp.zeros((NP + 2, TOP, CJ), F32)

    pl.semaphore_wait(barrier, expected)

    for d in range(1, low):
        pl.semaphore_signal(
            met, inc=1, device_id={"rows": peer_at(d), "cols": col}, device_id_type=MESH
        )

    def act_on(copy, act):
        if act == "start":
            copy.start()
        elif act == "send":
            copy.wait_send()
        else:
            copy.wait_recv()

    def col_copies(phase, act):
        place = pl.ds(TOP, L) if phase == 0 else pl.ds(0, L + 2 * TOP)
        for side, dc in ((0, 1), (1, -1)):
            copy = pltpu.make_async_remote_copy(
                src_ref=tmap.at[phase, NP if side == 0 else 1, place],
                dst_ref=tmap.at[phase, 0 if side == 0 else NP + 1, place],
                send_sem=col_ss.at[phase, side],
                recv_sem=col_rs.at[phase, side],
                device_id={"rows": row, "cols": col + (-dc if act == "recv" else dc)},
                device_id_type=MESH,
            )
            ok = col_ok[-dc] if act == "recv" else col_ok[dc]

            @pl.when(ok)
            def _():
                act_on(copy, act)

    def halo_copies(act):
        for way, dr in ((0, 1), (1, -1)):
            for slot in range(3):
                dc = slot - 1
                if act == "recv":
                    ok = jnp.logical_and(row_ok[-dr], col_ok[dc])
                    peer = {"rows": row - dr, "cols": col + dc}
                else:
                    ok = jnp.logical_and(row_ok[dr], col_ok[-dc])
                    peer = {"rows": row + dr, "cols": col - dc}
                copy = pltpu.make_async_remote_copy(
                    src_ref=edges.at[way],
                    dst_ref=halo.at[way, slot],
                    send_sem=halo_ss.at[way, slot],
                    recv_sem=halo_rs.at[way, slot],
                    device_id=peer,
                    device_id_type=MESH,
                )

                @pl.when(ok)
                def _():
                    act_on(copy, act)

    def edge_copies(act):
        for way, dr in ((0, 1), (1, -1)):
            copy = pltpu.make_async_remote_copy(
                src_ref=edges2.at[way],
                dst_ref=halo2.at[way],
                send_sem=h2_ss.at[way],
                recv_sem=h2_rs.at[way],
                device_id={"rows": row + (-dr if act == "recv" else dr), "cols": col},
                device_id_type=MESH,
            )

            @pl.when(row_ok[-dr] if act == "recv" else row_ok[dr])
            def _():
                act_on(copy, act)

    def exchange(act, source, target, send_sem, recv_sem):
        for d in range(R - 1, 0, -1):
            peer = peer_at(d)
            copy = pltpu.make_async_remote_copy(
                src_ref=source(peer),
                dst_ref=target.at[peer if act == "recv" else row],
                send_sem=send_sem.at[peer],
                recv_sem=recv_sem.at[peer if act == "recv" else row],
                device_id={"rows": peer, "cols": col},
                device_id_type=MESH,
            )
            act_on(copy, act)

    halo_copies("start")
    col_copies(0, "start")
    lane_place = iota((1, CJ), 1) % PATCH

    def rim_of(before, after):
        after = jnp.where(lane_place == 0, after, jnp.zeros_like(after))
        return jnp.where(lane_place == PATCH - 1, before, after)

    def conv(phase, blocks):
        count = len(blocks)
        near = sorted({p + d for p in blocks for d in range(3)})
        parts = []
        for b in range(3):
            rows = slice(TOP - 1 + b, TOP - 1 + b + L)
            cells = {p: tmap[phase, p, rows, :].astype(BF16) for p in near}
            parts.append(jnp.concatenate([cells[p + 1] for p in blocks], axis=0))
            rims = [rim_of(cells[p], cells[p + 2]) for p in blocks]
            parts.append(jnp.concatenate(rims, axis=0))
        total = dot(jnp.concatenate(parts, axis=1), taps[phase].reshape(6 * CJ, CJ))
        return total.reshape(count, L, CJ)

    def silu(v):
        return v * (0.5 + 0.5 * jnp.tanh(0.5 * v))

    embed_load.wait()
    for half in range(2):
        wide[half] = embed_v[:, half * LANES : (half + 1) * LANES].astype(F32)
    for i in range(PATCH):
        for half in range(2):
            embed_i[i, :, half * LANES : (half + 1) * LANES] = wide[
                half, pl.ds(i, CJ, stride=PATCH), :
            ].astype(BF16)

    edge_conv = ([None] * NP, [None] * NP)

    middle_blocks = list(range(1, NP - 1))
    outer_blocks = [0, NP - 1]

    def mix(blocks):
        inner = conv(0, blocks)
        for n, p in enumerate(blocks):
            base = tmap[0, p + 1, TOP : TOP + L, :]
            cells = (base + silu(inner[n])).astype(BF16).astype(F32)
            for half in range(2):
                mixed[half, p * L : (p + 1) * L, :] = cells[:, half * LANES : (half + 1) * LANES]
            edge_conv[0][p] = inner[n, 0:1, :]
            edge_conv[1][p] = inner[n, L - 1 : L, :]

    mix(middle_blocks)
    col_copies(0, "recv")
    if low > 1:
        pl.semaphore_wait(met, low - 1)
    k_source = lambda peer: sendk
    exchange("start", k_source, recvk, k_ss, k_rs)
    mix(outer_blocks)
    edge_conv = [jnp.concatenate(rows, axis=0) for rows in edge_conv]

    def embed(i, rows):
        return dot(rows.astype(BF16), embed_i[i])

    def normalise(tokens):
        mean = jnp.mean(tokens, axis=1, keepdims=True)
        centred = tokens - mean
        var = jnp.mean(centred * centred, axis=1, keepdims=True)
        return (centred * lax.rsqrt(var + EPSILON)).astype(BF16)

    cells = []
    for i in range(PATCH):
        halves = [mixed[half, pl.ds(i, NP * PR, stride=PATCH), :] for half in range(2)]
        cells.append(jnp.concatenate(halves, axis=1).astype(BF16))
    middle = dot(
        jnp.concatenate(cells[1 : PATCH - 1], axis=1),
        embed_i[1 : PATCH - 1].reshape((PATCH - 2) * CJ, D),
    )
    parts = {i: embed(i, cells[i]) for i in (0, PATCH - 1)}
    inner = (middle + parts[0] + parts[PATCH - 1]).astype(BF16).astype(F32)
    partial = (
        (middle + parts[PATCH - 1]).reshape(NP, PR, D)[:, 0, :],
        (middle + parts[0]).reshape(NP, PR, D)[:, PR - 1, :],
    )

    halo_copies("recv")
    edge_tokens = []
    for way, cell, tap in ((0, 0, 0), (1, L - 1, 2)):
        centre = halo[way, 1]
        before = jnp.concatenate([halo[way, 0, NP - 1 : NP, :], centre[0 : NP - 1]], axis=0)
        after = jnp.concatenate([centre[1:NP], halo[way, 2, 0:1, :]], axis=0)
        rim = rim_of(before, after)
        extra = dot(jnp.concatenate([centre, rim], axis=1).astype(BF16), taps[0, tap])
        fixed = (edges[1 - way] + silu(edge_conv[way] + extra)).astype(BF16).astype(F32)
        for half in range(2):
            mixed[half, pl.ds(cell, NP, stride=L), :] = fixed[:, half * LANES : (half + 1) * LANES]
        edge_token = partial[way] + embed(way * (PATCH - 1), fixed)
        edge_token = edge_token.astype(BF16).astype(F32)
        edge_tokens.append(edge_token)
        edges2[1 - way, 0:NP, :] = edge_token
        edges2[1 - way, NP : 2 * NP, :] = fixed
    place = iota((1, PR, 1), 1)
    tokens = jnp.where(
        place == 0,
        edge_tokens[0][:, None, :],
        jnp.where(place == PR - 1, edge_tokens[1][:, None, :], inner.reshape(NP, PR, D)),
    )

    qkv_load.wait()
    projected = dot(normalise(tokens.reshape(NP * PR, D)), qkv_v[...]).astype(BF16)
    for g in range(GH):
        for kind in range(3):
            start = kind * D + g * LANES
            part = projected[:, start : start + LANES].reshape(NP, PR, LANES)
            for p in range(NP):
                sendq[p * GH + g, :, kind * LANES : (kind + 1) * LANES] = part[p]
    q_source = lambda peer: sendq.at[peer // split]
    exchange("start", q_source, recvq, q_ss, q_rs)
    edge_copies("start")
    recvq[row] = sendq[row // split]
    recvk[row] = sendk[...]

    unp_load.wait()
    for k in range(PATCH):
        block = unp_v[:, k * CJ : (k + 1) * CJ].astype(F32).T
        for half in range(2):
            wide[half, k * CJ : (k + 1) * CJ, :] = block[:, half * LANES : (half + 1) * LANES]
    for i in range(PATCH):
        for half in range(2):
            unp_i[i, :, half * LANES : (half + 1) * LANES] = wide[
                half, pl.ds(i, CJ, stride=PATCH), :
            ].astype(BF16)

    cout_load.wait()
    banded(1, cout_v[...])
    outw_load.wait()
    exchange("recv", k_source, recvk, k_ss, k_rs)
    first_head = lax.rem(row, split) * my_heads
    first_global = (row // split) * group_heads + first_head
    pick = (iota((16, LANES), 1) == iota((16, LANES), 0) + first_global).astype(F32).astype(BF16)
    key_shift = dot_nt(pick, recvk[...].reshape(keys, LANES))
    exchange("recv", q_source, recvq, q_ss, q_rs)

    queries = recvq[:, :, 0:LANES].reshape(keys, LANES)
    none = jnp.zeros_like(queries)
    key_rows = recvq[:, :, LANES : 2 * LANES].reshape(keys, LANES)
    values = recvq[:, :, 2 * LANES : 3 * LANES].reshape(keys, LANES)
    lane_head = iota((1, LANES), 1) // HEAD_DIM
    softs, parts = [], []
    for k in range(my_heads):
        mine = lane_head == first_head + k
        query = jnp.where(mine, queries, none)
        scores = dot_nt(query, key_rows) * (HEAD_DIM**-0.5) + key_shift[k : k + 1, :]
        weights = jnp.exp(scores - jnp.max(scores, axis=1, keepdims=True))
        softs.append((weights * (1.0 / jnp.sum(weights, axis=1, keepdims=True))).astype(BF16))
        parts.append(jnp.where(mine, values, none))
    total = dot(jnp.concatenate(softs, axis=1), jnp.concatenate(parts, axis=0))
    total = total.reshape(R, PR, LANES)
    sendo[:, 0:PR, :] = total.astype(BF16)
    above = jnp.concatenate([total[R - 1 : R], total[0 : R - 1]], axis=0)[:, PR - 1 : PR, :]
    below = jnp.concatenate([total[1:R], total[0:1]], axis=0)[:, 0:1, :]
    sendo[:, PR : 2 * PR, :] = jnp.where(
        place == 0, above, jnp.where(place == 1, below, 0.0)
    ).astype(BF16)
    o_source = lambda peer: sendo.at[peer]
    exchange("start", o_source, recvo, o_ss, o_rs)
    recvo[row] = sendo[row]
    edge_copies("recv")
    halo_copies("send")
    col_copies(0, "send")
    exchange("send", k_source, recvk, k_ss, k_rs)
    exchange("send", q_source, recvq, q_ss, q_rs)
    edge_copies("send")
    exchange("recv", o_source, recvo, o_ss, o_rs)

    back = recvo[...].reshape(NP, GH, split, 2 * PR, LANES)
    sides = []
    for g in range(GH):
        share = back[:, g, 0]
        for s in range(1, split):
            share = share + back[:, g, s]
        sides.append(share.reshape(NP * 2 * PR, LANES))
    attended = jnp.concatenate(sides, axis=1)
    change = dot(attended, outw_v[...]).reshape(NP, 2 * PR, D)
    updated = (tokens + change[:, 0:PR, :]).reshape(NP * PR, D).astype(BF16)
    for way, i in ((0, PATCH - 1), (1, 0)):
        outer = (halo2[way, 0:NP, :] + change[:, PR + way, :]).astype(BF16)
        outer = halo2[way, NP : 2 * NP, :] + dot_nt(outer, unp_i[i])
        outer = jnp.where(row_ok[2 * way - 1], outer, 0.0).astype(BF16).astype(F32)
        for p in range(NP):
            tmap[1, p + 1, way * (TOP + L) : way * (TOP + L) + TOP, :] = jnp.broadcast_to(
                outer[p : p + 1, :], (TOP, CJ)
            )
    for i in range(PATCH):
        expanded = dot_nt(updated, unp_i[i])
        for half in range(2):
            wide[half, pl.ds(i, NP * PR, stride=PATCH), :] = expanded[
                :, half * LANES : (half + 1) * LANES
            ]

    def merge(p):
        for half in range(2):
            cells = mixed[half, p * L : (p + 1) * L, :] + wide[half, p * L : (p + 1) * L, :]
            tmap[1, p + 1, TOP : TOP + L, half * LANES : (half + 1) * LANES] = cells.astype(
                BF16
            ).astype(F32)

    merge(0)
    merge(NP - 1)
    col_copies(1, "start")
    for p in range(1, NP - 1):
        merge(p)
    exchange("send", o_source, recvo, o_ss, o_rs)

    def finish(blocks, second):
        return {
            p: (tmap[1, p + 1, TOP : TOP + L, :] + second[n]).T.reshape(C, PATCH, L)
            for n, p in enumerate(blocks)
        }

    def put(q, top, bottom):
        o_ref[:, 2 * PATCH * q : 2 * PATCH * (q + 1), :] = jnp.concatenate(
            [top, bottom], axis=1
        ).astype(BF16)

    inside = conv(1, middle_blocks)
    col_copies(1, "recv")
    outside = conv(1, outer_blocks)
    done = finish(middle_blocks, inside) | finish(outer_blocks, outside)
    for q in range(NP // 2):
        put(q, done[2 * q], done[2 * q + 1])
    col_copies(1, "send")


def per_device(
    R, NC, pair_map, conv_in, embed_weight, qkv_weight, key_bias, out_weight, unpatch, conv_out
):
    NP = pair_map.shape[1] // PATCH
    L = pair_map.shape[2]
    PR = L // PATCH
    CJ = C * PATCH
    groups = NP * (D // LANES)
    hbm = pl.BlockSpec(memory_space=pltpu.HBM)
    dma = pltpu.SemaphoreType.DMA
    inputs = (
        pair_map,
        key_bias.transpose(1, 2, 0),
        conv_in,
        conv_out,
        embed_weight,
        qkv_weight,
        out_weight,
        unpatch,
    )
    return pl.pallas_call(
        functools.partial(trunk_kernel, R, NC),
        out_shape=pltpu.VMEM(pair_map.shape, BF16),
        in_specs=[hbm] * 8,
        out_specs=pl.BlockSpec(memory_space=pltpu.VMEM),
        scratch_shapes=[pltpu.VMEM(a.shape, BF16) for a in inputs]
        + [
            pltpu.VMEM((2, NP + 2, L + 2 * TOP, CJ), F32),
            pltpu.VMEM((2, NP * L, LANES), F32),
            pltpu.VMEM((2, NP, CJ), F32),
            pltpu.VMEM((2, 3, NP, CJ), F32),
            pltpu.VMEM((2, 2 * NP, CJ), F32),
            pltpu.VMEM((2, 2 * NP, CJ), F32),
            pltpu.VMEM((2, CJ * PATCH, LANES), F32),
            pltpu.VMEM((PATCH, CJ, D), BF16),
            pltpu.VMEM((PATCH, CJ, D), BF16),
            pltpu.VMEM((2, 3, 2 * CJ, CJ), BF16),
            pltpu.VMEM((PR, LANES), BF16),
            pltpu.VMEM((R, PR, LANES), BF16),
            pltpu.VMEM((groups, PR, 3 * LANES), BF16),
            pltpu.VMEM((R, PR, 3 * LANES), BF16),
            pltpu.VMEM((R, 2 * PR, LANES), BF16),
            pltpu.VMEM((R, 2 * PR, LANES), BF16),
            dma((NP // 2,)),
            dma((7,)),
            dma((2, 3)),
            dma((2, 3)),
            dma((2, 2)),
            dma((2, 2)),
            dma((2,)),
            dma((2,)),
            dma((R,)),
            dma((R,)),
            dma((R,)),
            dma((R,)),
            dma((R,)),
            dma((R,)),
            pltpu.SemaphoreType.REGULAR,
        ],
        compiler_params=pltpu.CompilerParams(
            collective_id=0, has_side_effects=True, vmem_limit_bytes=VMEM_BYTES
        ),
    )(*inputs)


def solution(mesh):
    placed = (P(None, "cols", "rows"), P(), P(), P(), P("rows", "cols", None), P(), P(), P())
    return jax.shard_map(
        functools.partial(per_device, mesh.shape["rows"], mesh.shape["cols"]),
        mesh=mesh,
        in_specs=placed,
        out_specs=P(None, "cols", "rows"),
        check_vma=False,
    )
```

```python
import functools

import jax
import jax.numpy as jnp
from jax import lax
from jax.experimental import pallas as pl
from jax.experimental.pallas import tpu as pltpu
from jax.sharding import PartitionSpec as P

C = 32
PATCH = 8
D = 256
HEADS = 8
HEAD_DIM = 32
LANES = 128
EPSILON = 1e-05
F32 = jnp.float32
BF16 = jnp.bfloat16
MESH = pl.DeviceIdType.MESH
NT = (((1,), (1,)), ((), ()))
TOP = 8
VMEM_BYTES = 56 * 1024 * 1024


def dot(a, b):
    return jnp.dot(a, b, preferred_element_type=F32)


def dot_nt(a, b):
    return lax.dot_general(a, b, NT, preferred_element_type=F32)


def iota(shape, dim):
    return lax.broadcasted_iota(jnp.int32, shape, dim)


def trunk_kernel(
    R,
    NC,
    x_hbm,
    kb_hbm,
    cin_hbm,
    cout_hbm,
    embed_hbm,
    qkv_hbm,
    outw_hbm,
    unp_hbm,
    o_ref,
    x_v,
    kb_v,
    cin_v,
    cout_v,
    embed_v,
    qkv_v,
    outw_v,
    unp_v,
    tmap,
    mixed,
    edges,
    halo,
    edges2,
    halo2,
    wide,
    embed_i,
    unp_i,
    taps,
    sendk,
    recvk,
    sendq,
    recvq,
    sendo,
    recvo,
    x_sem,
    load_sem,
    halo_ss,
    halo_rs,
    col_ss,
    col_rs,
    h2_ss,
    h2_rs,
    k_ss,
    k_rs,
    q_ss,
    q_rs,
    o_ss,
    o_rs,
    met,
):
    row = lax.axis_index("rows")
    col = lax.axis_index("cols")
    NP = x_v.shape[1] // PATCH
    L = x_v.shape[2]
    PR = L // PATCH
    CJ = C * PATCH
    GH = D // LANES
    groups = NP * GH
    split = R // groups
    group_heads = LANES // HEAD_DIM
    my_heads = group_heads // split
    keys = R * PR
    bits = R.bit_length() - 1
    low = 2 ** (bits // 2)

    row_ok = {-1: row > 0, 1: row < R - 1}
    col_ok = {-1: col > 0, 0: col >= 0, 1: col < NC - 1}
    barrier = pltpu.get_barrier_semaphore()

    def partner(k):
        return row + (1 - 2 * lax.rem(row // 2**k, 2)) * 2**k

    flips = [partner(k) - row for k in range(bits)]

    def peer_at(d):
        peer = row
        for k in range(bits):
            if d // 2**k % 2:
                peer = peer + flips[k]
        return peer

    def greet(peer_row, peer_col):
        pl.semaphore_signal(
            barrier,
            inc=1,
            device_id={"rows": peer_row, "cols": peer_col},
            device_id_type=MESH,
        )

    lines = list(range(R - low, 0, -low)) + list(range(low - 1, 0, -1))
    for d in lines:
        greet(peer_at(d), col)
    expected = len(lines)
    for dr in (-1, 1):
        expected = expected + row_ok[dr].astype(jnp.int32)

        @pl.when(row_ok[dr])
        def _():
            greet(row + dr, col)

    for dc in (-1, 1):
        for dr in (-1, 0, 1):
            ok = col_ok[dc] if dr == 0 else jnp.logical_and(col_ok[dc], row_ok[dr])
            expected = expected + ok.astype(jnp.int32)

            @pl.when(ok)
            def _():
                greet(row + dr, col + dc)

    x_loads = [
        pltpu.make_async_copy(
            x_hbm.at[:, pl.ds(2 * PATCH * q, 2 * PATCH), :],
            x_v.at[:, pl.ds(2 * PATCH * q, 2 * PATCH), :],
            x_sem.at[q],
        )
        for q in range(NP // 2)
    ]
    loads = [
        pltpu.make_async_copy(src, dst, load_sem.at[n])
        for n, (src, dst) in enumerate(
            (
                (cin_hbm, cin_v),
                (embed_hbm, embed_v),
                (kb_hbm, kb_v),
                (qkv_hbm, qkv_v),
                (unp_hbm, unp_v),
                (cout_hbm, cout_v),
                (outw_hbm, outw_v),
            )
        )
    ]
    cin_load, embed_load, kb_load, qkv_load, unp_load, cout_load, outw_load = loads
    for copy in (cin_load, kb_load, *x_loads, embed_load, qkv_load, unp_load, cout_load, outw_load):
        copy.start()

    def banded(n, weight):
        spread = (iota((CJ, C), 0) // PATCH == iota((CJ, C), 1)).astype(F32).astype(BF16)
        wide_weight = dot(spread, weight).astype(BF16)
        shift = iota((CJ, CJ), 0) % PATCH - iota((CJ, CJ), 1) % PATCH
        ahead = iota((CJ, 9 * C), 1) - iota((CJ, 9 * C), 0) // PATCH
        for b in range(3):
            centre = jnp.zeros((CJ, CJ), F32)
            rim = jnp.zeros((CJ, CJ), F32)
            for a in range(3):
                start = (3 * a + b) * C
                lanes = slice(0, CJ) if start < CJ else slice(CJ, 9 * C)
                pick = (ahead[:, lanes] == start).astype(F32).astype(BF16)
                full = dot_nt(pick, wide_weight[:, lanes])
                centre = jnp.where(shift == a - 1, full, centre)
                if a == 0:
                    rim = jnp.where(shift == PATCH - 1, full, rim)
                if a == 2:
                    rim = jnp.where(shift == 1 - PATCH, full, rim)
            taps[n, b, 0:CJ, :] = centre.astype(BF16)
            taps[n, b, CJ : 2 * CJ, :] = rim.astype(BF16)

    cin_load.wait()
    banded(0, cin_v[...])

    kb_load.wait()
    same = (iota((PR, PR), 0) == iota((PR, PR), 1)).astype(F32).astype(BF16)
    bias = dot_nt(same, kb_v[...].astype(F32).reshape(NP * HEADS, PR).astype(BF16))
    pad = jnp.zeros((PR, LANES - NP * HEADS), F32)
    sendk[...] = jnp.concatenate([bias, pad], axis=1).astype(BF16)

    for q in range(NP // 2):
        x_loads[q].wait()
        pair = x_v[:, 2 * PATCH * q : 2 * PATCH * (q + 1), :].astype(F32)
        for s in range(2):
            block = pair[:, PATCH * s : PATCH * (s + 1), :].reshape(CJ, L)
            tmap[0, 1 + 2 * q + s, TOP : TOP + L, :] = block.T
    for p in range(NP):
        edges[0, p : p + 1, :] = tmap[0, p + 1, TOP + L - 1 : TOP + L, :]
        edges[1, p : p + 1, :] = tmap[0, p + 1, TOP : TOP + 1, :]

    for way, dr in ((0, -1), (1, 1)):
        for slot in range(3):
            missing = jnp.logical_not(jnp.logical_and(row_ok[dr], col_ok[slot - 1]))

            @pl.when(missing)
            def _():
                halo[way, slot] = jnp.zeros((NP, CJ), F32)

        @pl.when(jnp.logical_not(row_ok[dr]))
        def _():
            halo2[way] = jnp.zeros((2 * NP, CJ), F32)

    for side, dc in ((0, -1), (1, 1)):

        @pl.when(jnp.logical_not(col_ok[dc]))
        def _():
            tmap[0, side * (NP + 1), TOP : TOP + L, :] = jnp.zeros((L, CJ), F32)
            tmap[1, side * (NP + 1), :, :] = jnp.zeros((L + 2 * TOP, CJ), F32)

    tmap[0, :, 0:TOP, :] = jnp.zeros((NP + 2, TOP, CJ), F32)
    tmap[0, :, TOP + L : L + 2 * TOP, :] = jnp.zeros((NP + 2, TOP, CJ), F32)

    pl.semaphore_wait(barrier, expected)

    for d in range(1, low):
        pl.semaphore_signal(
            met, inc=1, device_id={"rows": peer_at(d), "cols": col}, device_id_type=MESH
        )

    def act_on(copy, act):
        if act == "start":
            copy.start()
        elif act == "send":
            copy.wait_send()
        else:
            copy.wait_recv()

    def col_copies(phase, act):
        place = pl.ds(TOP, L) if phase == 0 else pl.ds(0, L + 2 * TOP)
        for side, dc in ((0, 1), (1, -1)):
            copy = pltpu.make_async_remote_copy(
                src_ref=tmap.at[phase, NP if side == 0 else 1, place],
                dst_ref=tmap.at[phase, 0 if side == 0 else NP + 1, place],
                send_sem=col_ss.at[phase, side],
                recv_sem=col_rs.at[phase, side],
                device_id={"rows": row, "cols": col + (-dc if act == "recv" else dc)},
                device_id_type=MESH,
            )
            ok = col_ok[-dc] if act == "recv" else col_ok[dc]

            @pl.when(ok)
            def _():
                act_on(copy, act)

    def halo_copies(act):
        for way, dr in ((0, 1), (1, -1)):
            for slot in range(3):
                dc = slot - 1
                if act == "recv":
                    ok = jnp.logical_and(row_ok[-dr], col_ok[dc])
                    peer = {"rows": row - dr, "cols": col + dc}
                else:
                    ok = jnp.logical_and(row_ok[dr], col_ok[-dc])
                    peer = {"rows": row + dr, "cols": col - dc}
                copy = pltpu.make_async_remote_copy(
                    src_ref=edges.at[way],
                    dst_ref=halo.at[way, slot],
                    send_sem=halo_ss.at[way, slot],
                    recv_sem=halo_rs.at[way, slot],
                    device_id=peer,
                    device_id_type=MESH,
                )

                @pl.when(ok)
                def _():
                    act_on(copy, act)

    def edge_copies(act):
        for way, dr in ((0, 1), (1, -1)):
            copy = pltpu.make_async_remote_copy(
                src_ref=edges2.at[way],
                dst_ref=halo2.at[way],
                send_sem=h2_ss.at[way],
                recv_sem=h2_rs.at[way],
                device_id={"rows": row + (-dr if act == "recv" else dr), "cols": col},
                device_id_type=MESH,
            )

            @pl.when(row_ok[-dr] if act == "recv" else row_ok[dr])
            def _():
                act_on(copy, act)

    def exchange(act, source, target, send_sem, recv_sem):
        order = sorted(range(1, R), key=lambda d: (d // (R // 2), d % (R // 4), d), reverse=True)
        for d in order:
            peer = peer_at(d)
            copy = pltpu.make_async_remote_copy(
                src_ref=source(peer),
                dst_ref=target.at[peer if act == "recv" else row],
                send_sem=send_sem.at[peer],
                recv_sem=recv_sem.at[peer if act == "recv" else row],
                device_id={"rows": peer, "cols": col},
                device_id_type=MESH,
            )
            act_on(copy, act)

    halo_copies("start")
    col_copies(0, "start")
    lane_place = iota((1, CJ), 1) % PATCH

    def rim_of(before, after):
        after = jnp.where(lane_place == 0, after, jnp.zeros_like(after))
        return jnp.where(lane_place == PATCH - 1, before, after)

    def conv(phase, blocks):
        count = len(blocks)
        near = sorted({p + d for p in blocks for d in range(3)})
        parts = []
        for b in range(3):
            rows = slice(TOP - 1 + b, TOP - 1 + b + L)
            cells = {p: tmap[phase, p, rows, :].astype(BF16) for p in near}
            parts.append(jnp.concatenate([cells[p + 1] for p in blocks], axis=0))
            rims = [rim_of(cells[p], cells[p + 2]) for p in blocks]
            parts.append(jnp.concatenate(rims, axis=0))
        total = dot(jnp.concatenate(parts, axis=1), taps[phase].reshape(6 * CJ, CJ))
        return total.reshape(count, L, CJ)

    def silu(v):
        return v * (0.5 + 0.5 * jnp.tanh(0.5 * v))

    embed_load.wait()
    for half in range(2):
        wide[half] = embed_v[:, half * LANES : (half + 1) * LANES].astype(F32)
    for i in range(PATCH):
        for half in range(2):
            embed_i[i, :, half * LANES : (half + 1) * LANES] = wide[
                half, pl.ds(i, CJ, stride=PATCH), :
            ].astype(BF16)

    edge_conv = ([None] * NP, [None] * NP)

    middle_blocks = list(range(1, NP - 1))
    outer_blocks = [0, NP - 1]

    def mix(blocks):
        inner = conv(0, blocks)
        for n, p in enumerate(blocks):
            base = tmap[0, p + 1, TOP : TOP + L, :]
            cells = (base + silu(inner[n])).astype(BF16).astype(F32)
            for half in range(2):
                mixed[half, p * L : (p + 1) * L, :] = cells[:, half * LANES : (half + 1) * LANES]
            edge_conv[0][p] = inner[n, 0:1, :]
            edge_conv[1][p] = inner[n, L - 1 : L, :]

    mix(middle_blocks)
    col_copies(0, "recv")
    if low > 1:
        pl.semaphore_wait(met, low - 1)
    k_source = lambda peer: sendk
    exchange("start", k_source, recvk, k_ss, k_rs)
    mix(outer_blocks)
    edge_conv = [jnp.concatenate(rows, axis=0) for rows in edge_conv]

    def embed(i, rows):
        return dot(rows.astype(BF16), embed_i[i])

    def normalise(tokens):
        mean = jnp.mean(tokens, axis=1, keepdims=True)
        centred = tokens - mean
        var = jnp.mean(centred * centred, axis=1, keepdims=True)
        return (centred * lax.rsqrt(var + EPSILON)).astype(BF16)

    cells = []
    for i in range(PATCH):
        halves = [mixed[half, pl.ds(i, NP * PR, stride=PATCH), :] for half in range(2)]
        cells.append(jnp.concatenate(halves, axis=1).astype(BF16))
    middle = dot(
        jnp.concatenate(cells[1 : PATCH - 1], axis=1),
        embed_i[1 : PATCH - 1].reshape((PATCH - 2) * CJ, D),
    )
    parts = {i: embed(i, cells[i]) for i in (0, PATCH - 1)}
    inner = (middle + parts[0] + parts[PATCH - 1]).astype(BF16).astype(F32)
    partial = (
        (middle + parts[PATCH - 1]).reshape(NP, PR, D)[:, 0, :],
        (middle + parts[0]).reshape(NP, PR, D)[:, PR - 1, :],
    )

    halo_copies("recv")
    edge_tokens = []
    for way, cell, tap in ((0, 0, 0), (1, L - 1, 2)):
        centre = halo[way, 1]
        before = jnp.concatenate([halo[way, 0, NP - 1 : NP, :], centre[0 : NP - 1]], axis=0)
        after = jnp.concatenate([centre[1:NP], halo[way, 2, 0:1, :]], axis=0)
        rim = rim_of(before, after)
        extra = dot(jnp.concatenate([centre, rim], axis=1).astype(BF16), taps[0, tap])
        fixed = (edges[1 - way] + silu(edge_conv[way] + extra)).astype(BF16).astype(F32)
        for half in range(2):
            mixed[half, pl.ds(cell, NP, stride=L), :] = fixed[:, half * LANES : (half + 1) * LANES]
        edge_token = partial[way] + embed(way * (PATCH - 1), fixed)
        edge_token = edge_token.astype(BF16).astype(F32)
        edge_tokens.append(edge_token)
        edges2[1 - way, 0:NP, :] = edge_token
        edges2[1 - way, NP : 2 * NP, :] = fixed
    place = iota((1, PR, 1), 1)
    tokens = jnp.where(
        place == 0,
        edge_tokens[0][:, None, :],
        jnp.where(place == PR - 1, edge_tokens[1][:, None, :], inner.reshape(NP, PR, D)),
    )

    qkv_load.wait()
    projected = dot(normalise(tokens.reshape(NP * PR, D)), qkv_v[...]).astype(BF16)
    for g in range(GH):
        for kind in range(3):
            start = kind * D + g * LANES
            part = projected[:, start : start + LANES].reshape(NP, PR, LANES)
            for p in range(NP):
                sendq[p * GH + g, :, kind * LANES : (kind + 1) * LANES] = part[p]
    q_source = lambda peer: sendq.at[peer // split]
    exchange("start", q_source, recvq, q_ss, q_rs)
    edge_copies("start")
    recvq[row] = sendq[row // split]
    recvk[row] = sendk[...]

    unp_load.wait()
    for k in range(PATCH):
        block = unp_v[:, k * CJ : (k + 1) * CJ].astype(F32).T
        for half in range(2):
            wide[half, k * CJ : (k + 1) * CJ, :] = block[:, half * LANES : (half + 1) * LANES]
    for i in range(PATCH):
        for half in range(2):
            unp_i[i, :, half * LANES : (half + 1) * LANES] = wide[
                half, pl.ds(i, CJ, stride=PATCH), :
            ].astype(BF16)

    cout_load.wait()
    banded(1, cout_v[...])
    outw_load.wait()
    exchange("recv", k_source, recvk, k_ss, k_rs)
    first_head = lax.rem(row, split) * my_heads
    first_global = (row // split) * group_heads + first_head
    pick = (iota((16, LANES), 1) == iota((16, LANES), 0) + first_global).astype(F32).astype(BF16)
    key_shift = dot_nt(pick, recvk[...].reshape(keys, LANES))
    exchange("recv", q_source, recvq, q_ss, q_rs)

    queries = recvq[:, :, 0:LANES].reshape(keys, LANES)
    none = jnp.zeros_like(queries)
    key_rows = recvq[:, :, LANES : 2 * LANES].reshape(keys, LANES)
    values = recvq[:, :, 2 * LANES : 3 * LANES].reshape(keys, LANES)
    lane_head = iota((1, LANES), 1) // HEAD_DIM
    softs, parts = [], []
    for k in range(my_heads):
        mine = lane_head == first_head + k
        query = jnp.where(mine, queries, none)
        scores = dot_nt(query, key_rows) * (HEAD_DIM**-0.5) + key_shift[k : k + 1, :]
        weights = jnp.exp(scores - jnp.max(scores, axis=1, keepdims=True))
        softs.append((weights * (1.0 / jnp.sum(weights, axis=1, keepdims=True))).astype(BF16))
        parts.append(jnp.where(mine, values, none))
    total = dot(jnp.concatenate(softs, axis=1), jnp.concatenate(parts, axis=0))
    total = total.reshape(R, PR, LANES)
    sendo[:, 0:PR, :] = total.astype(BF16)
    above = jnp.concatenate([total[R - 1 : R], total[0 : R - 1]], axis=0)[:, PR - 1 : PR, :]
    below = jnp.concatenate([total[1:R], total[0:1]], axis=0)[:, 0:1, :]
    sendo[:, PR : 2 * PR, :] = jnp.where(
        place == 0, above, jnp.where(place == 1, below, 0.0)
    ).astype(BF16)
    o_source = lambda peer: sendo.at[peer]
    exchange("start", o_source, recvo, o_ss, o_rs)
    recvo[row] = sendo[row]
    edge_copies("recv")
    halo_copies("send")
    col_copies(0, "send")
    exchange("send", k_source, recvk, k_ss, k_rs)
    exchange("send", q_source, recvq, q_ss, q_rs)
    edge_copies("send")
    exchange("recv", o_source, recvo, o_ss, o_rs)

    back = recvo[...].reshape(NP, GH, split, 2 * PR, LANES)
    sides = []
    for g in range(GH):
        share = back[:, g, 0]
        for s in range(1, split):
            share = share + back[:, g, s]
        sides.append(share.reshape(NP * 2 * PR, LANES))
    attended = jnp.concatenate(sides, axis=1)
    change = dot(attended, outw_v[...]).reshape(NP, 2 * PR, D)
    updated = (tokens + change[:, 0:PR, :]).reshape(NP * PR, D).astype(BF16)
    for way, i in ((0, PATCH - 1), (1, 0)):
        outer = (halo2[way, 0:NP, :] + change[:, PR + way, :]).astype(BF16)
        outer = halo2[way, NP : 2 * NP, :] + dot_nt(outer, unp_i[i])
        outer = jnp.where(row_ok[2 * way - 1], outer, 0.0).astype(BF16).astype(F32)
        for p in range(NP):
            tmap[1, p + 1, way * (TOP + L) : way * (TOP + L) + TOP, :] = jnp.broadcast_to(
                outer[p : p + 1, :], (TOP, CJ)
            )
    for i in range(PATCH):
        expanded = dot_nt(updated, unp_i[i])
        for half in range(2):
            wide[half, pl.ds(i, NP * PR, stride=PATCH), :] = expanded[
                :, half * LANES : (half + 1) * LANES
            ]

    def merge(p):
        for half in range(2):
            cells = mixed[half, p * L : (p + 1) * L, :] + wide[half, p * L : (p + 1) * L, :]
            tmap[1, p + 1, TOP : TOP + L, half * LANES : (half + 1) * LANES] = cells.astype(
                BF16
            ).astype(F32)

    merge(0)
    merge(NP - 1)
    col_copies(1, "start")
    for p in range(1, NP - 1):
        merge(p)
    exchange("send", o_source, recvo, o_ss, o_rs)

    def finish(blocks, second):
        return {
            p: (tmap[1, p + 1, TOP : TOP + L, :] + second[n]).T.reshape(C, PATCH, L)
            for n, p in enumerate(blocks)
        }

    def put(q, top, bottom):
        o_ref[:, 2 * PATCH * q : 2 * PATCH * (q + 1), :] = jnp.concatenate(
            [top, bottom], axis=1
        ).astype(BF16)

    inside = conv(1, middle_blocks)
    col_copies(1, "recv")
    outside = conv(1, outer_blocks)
    done = finish(middle_blocks, inside) | finish(outer_blocks, outside)
    for q in range(NP // 2):
        put(q, done[2 * q], done[2 * q + 1])
    col_copies(1, "send")


def per_device(
    R, NC, pair_map, conv_in, embed_weight, qkv_weight, key_bias, out_weight, unpatch, conv_out
):
    NP = pair_map.shape[1] // PATCH
    L = pair_map.shape[2]
    PR = L // PATCH
    CJ = C * PATCH
    groups = NP * (D // LANES)
    hbm = pl.BlockSpec(memory_space=pltpu.HBM)
    dma = pltpu.SemaphoreType.DMA
    inputs = (
        pair_map,
        key_bias.transpose(1, 2, 0),
        conv_in,
        conv_out,
        embed_weight,
        qkv_weight,
        out_weight,
        unpatch,
    )
    return pl.pallas_call(
        functools.partial(trunk_kernel, R, NC),
        out_shape=pltpu.VMEM(pair_map.shape, BF16),
        in_specs=[hbm] * 8,
        out_specs=pl.BlockSpec(memory_space=pltpu.VMEM),
        scratch_shapes=[pltpu.VMEM(a.shape, BF16) for a in inputs]
        + [
            pltpu.VMEM((2, NP + 2, L + 2 * TOP, CJ), F32),
            pltpu.VMEM((2, NP * L, LANES), F32),
            pltpu.VMEM((2, NP, CJ), F32),
            pltpu.VMEM((2, 3, NP, CJ), F32),
            pltpu.VMEM((2, 2 * NP, CJ), F32),
            pltpu.VMEM((2, 2 * NP, CJ), F32),
            pltpu.VMEM((2, CJ * PATCH, LANES), F32),
            pltpu.VMEM((PATCH, CJ, D), BF16),
            pltpu.VMEM((PATCH, CJ, D), BF16),
            pltpu.VMEM((2, 3, 2 * CJ, CJ), BF16),
            pltpu.VMEM((PR, LANES), BF16),
            pltpu.VMEM((R, PR, LANES), BF16),
            pltpu.VMEM((groups, PR, 3 * LANES), BF16),
            pltpu.VMEM((R, PR, 3 * LANES), BF16),
            pltpu.VMEM((R, 2 * PR, LANES), BF16),
            pltpu.VMEM((R, 2 * PR, LANES), BF16),
            dma((NP // 2,)),
            dma((7,)),
            dma((2, 3)),
            dma((2, 3)),
            dma((2, 2)),
            dma((2, 2)),
            dma((2,)),
            dma((2,)),
            dma((R,)),
            dma((R,)),
            dma((R,)),
            dma((R,)),
            dma((R,)),
            dma((R,)),
            pltpu.SemaphoreType.REGULAR,
        ],
        compiler_params=pltpu.CompilerParams(
            collective_id=0, has_side_effects=True, vmem_limit_bytes=VMEM_BYTES
        ),
    )(*inputs)


def solution(mesh):
    placed = (P(None, "cols", "rows"), P(), P(), P(), P("rows", "cols", None), P(), P(), P())
    return jax.shard_map(
        functools.partial(per_device, mesh.shape["rows"], mesh.shape["cols"]),
        mesh=mesh,
        in_specs=placed,
        out_specs=P(None, "cols", "rows"),
        check_vma=False,
    )
```
